256 devices in a mesh: lon: 32 (over z, x_hi, core), lat: 8 (over y, x_lo).
Axes of the slice: x: 4 (x_hi: 2, x_lo: 2; x = x_hi * 2 + x_lo), y: 4, z: 8, core: 2. Of those that a mesh axis runs over, the one named last changes fastest.
Arguments:
- field: bfloat16 [32, 1024, 256], P('lat', 'lon'), may hold values from -6 to 6
- cotangent: bfloat16 [32, 1024, 256], P('lat', 'lon'), may hold values from -6 to 6
- mix_weight: bfloat16 [256, 256], replicated, may hold values from -0.375 to 0.375
- first_weight: float32 [3, 256], replicated, may hold values from -0.34 to 0.34
- first_bias: float32 [256], replicated, may hold values from -0.5 to 0.5
- hidden_weight: bfloat16 [256, 256], replicated, may hold values from -0.375 to 0.375
- hidden_bias: float32 [256], replicated, may hold values from -1 to 1
- output_weight: bfloat16 [256, 256], replicated, may hold values from -0.375 to 0.375
- output_bias: float32 [256], replicated, may hold values from -0.5 to 0.5
- lon_half: int32 [32], replicated, may hold values from 3 to 32, as said below
- lat_half: int32 [32], replicated, may hold values from 1 to 4, as said below
Outputs:
- grad_field: bfloat16 [32, 1024, 256], P('lat', 'lon')
- grad_mix: float32 [256, 256], replicated
- grad_first_weight: float32 [3, 256], replicated
- grad_first_bias: float32 [256], replicated
- grad_hidden_weight: float32 [256, 256], replicated
- grad_hidden_bias: float32 [256], replicated
- grad_output_weight: float32 [256, 256], replicated
- grad_output_bias: float32 [256], replicated
The draws below stay inside these ranges and needn't reach their ends.
Inputs may be any that keep to these rules, and one draw needn't show every extreme that they name: lon_half[i] is row i's half-width in longitude: 32 in the first and last rows. lat_half[i] is row i's half-width in latitude: 4 in the first and last rows.
All inputs are finite; a program needn't handle non-finite values.
Results may differ from the reference program's by a relative error of at most 0.0064.
Values may be sent and summed in bfloat16 or wider, within the bound.
No kernel may reach another device: no remote copies, remote signals or barrier semaphores. Data moves between devices by JAX's collectives and lax.ppermute only.
A program may use at most 128 MiB of HBM per device.

```python
import math
import jax
import jax.numpy as jnp
from jax import lax

C = 256
HID = 256
HLON = 32
HLAT = 4
NLAT = 32
NLON = 1024


def edge_distance():
    row_index = jnp.arange(NLAT)
    return jnp.minimum(row_index, NLAT - 1 - row_index)


def draw_lon_half(key, part):
    distance = edge_distance()
    widths = 3 * NLAT // (2 * distance + 1)
    jitter = jax.random.randint(jax.random.fold_in(key, 11), (NLAT,), 0, 5)
    widths = jnp.clip(widths + jitter, 3, HLON)
    return jnp.where(distance == 0, HLON, widths).astype(jnp.int32)


def draw_lat_half(key, part):
    distance = edge_distance()
    widths = jax.random.randint(jax.random.fold_in(key, 23), (NLAT,), 1, HLAT + 1)
    return jnp.where(distance == 0, HLAT, widths).astype(jnp.int32)


def block_scale(stream_key, dims, split, smallest, largest):
    def one(position, parts):
        heights = jax.random.uniform(jax.random.fold_in(jax.random.fold_in(stream_key, 6), position), (parts,), jnp.float32, smallest / len(split), largest / len(split))
        return jnp.repeat(jnp.exp(heights), dims[position] // parts).reshape((-1,) + (1,) * (len(dims) - position - 1))

    factor_of = one(*split[0])
    for cut in split[1:]:
        factor_of = factor_of * one(*cut)
    return factor_of


def gaussian(stream_key, dims, scale, limit, cuts=(), dtype=jnp.bfloat16):
    values = scale * jax.random.normal(stream_key, dims, jnp.float32)
    if cuts:
        values = values * block_scale(stream_key, dims, cuts, -0.22, 0.18)
    return jnp.clip(values, -limit, limit).astype(dtype)


def setup_inputs(seed: int = 0) -> dict:
    key_of = jax.random.split(jax.random.key(seed), 12)
    field = gaussian(key_of[0], (NLAT, NLON, C), 1.0, 6.0, ((0, 8), (1, 32)))
    cotangent = gaussian(key_of[1], (NLAT, NLON, C), 1.0, 6.0, ((0, 8), (1, 32)))
    mix_weight = gaussian(key_of[2], (C, C), C ** -0.5, 0.375)
    first_weight = jnp.clip(jax.random.uniform(key_of[3], (3, HID), jnp.float32, -0.34, 0.34), -0.34, 0.34)
    first_bias = jnp.clip(jax.random.uniform(key_of[4], (HID,), jnp.float32, -0.5, 0.5), -0.5, 0.5)
    hidden_weight = gaussian(key_of[5], (HID, HID), HID ** -0.5, 0.375)
    hidden_bias = jnp.clip(jax.random.uniform(key_of[6], (HID,), jnp.float32, -1.0, 1.0), -1.0, 1.0)
    output_weight = gaussian(key_of[7], (HID, C), HID ** -0.5, 0.375)
    output_bias = jnp.clip(jax.random.uniform(key_of[8], (C,), jnp.float32, -0.5, 0.5), -0.5, 0.5)
    lon_half = draw_lon_half(jax.random.fold_in(key_of[11], 71), 0)
    lat_half = draw_lat_half(jax.random.fold_in(key_of[11], 71), 0)
    return dict(field=field, cotangent=cotangent, mix_weight=mix_weight, first_weight=first_weight, first_bias=first_bias, hidden_weight=hidden_weight, hidden_bias=hidden_bias, output_weight=output_weight, output_bias=output_bias, lon_half=lon_half, lat_half=lat_half)


first_omega = 30.0

def tap_setup(lon_half, lat_half):
    taps_lon = 2 * HLON + 1
    taps_lat = 2 * HLAT + 1
    row_index = jnp.arange(NLAT).astype(jnp.float32)
    shift_lon = jnp.arange(taps_lon) - HLON
    shift_lat = jnp.arange(taps_lat) - HLAT
    half_lon = lon_half[:, None, None]
    half_lat = lat_half[:, None, None]
    shape = (NLAT, taps_lon, taps_lat)
    lon_coord = jnp.broadcast_to(shift_lon[None, :, None].astype(jnp.float32) / half_lon.astype(jnp.float32), shape)
    lat_coord = jnp.broadcast_to(shift_lat[None, None, :].astype(jnp.float32) / half_lat.astype(jnp.float32), shape)
    lat_sine = jnp.broadcast_to(jnp.sin(jnp.pi * ((row_index + 0.5) / NLAT - 0.5))[:, None, None], shape)
    inside = (jnp.abs(shift_lon)[None, :, None] <= half_lon) & (jnp.abs(shift_lat)[None, None, :] <= half_lat)
    row_norm = lax.rsqrt(((2 * lon_half + 1) * (2 * lat_half + 1)).astype(jnp.float32))
    tap_scale = jnp.where(inside, jnp.broadcast_to(row_norm[:, None, None], shape), jnp.zeros(shape, jnp.float32))
    return (lon_coord, lat_coord, lat_sine, tap_scale)

def reference(field, cotangent, mix_weight, first_weight, first_bias, hidden_weight, hidden_bias, output_weight, output_bias, lon_half, lat_half):
    highest = lax.Precision.HIGHEST
    taps_lon = 2 * HLON + 1
    taps_lat = 2 * HLAT + 1
    lon_coord, lat_coord, lat_sine, tap_scale = tap_setup(lon_half, lat_half)
    pre_first = lon_coord[..., None] * first_weight[0] + lat_coord[..., None] * first_weight[1] + lat_sine[..., None] * first_weight[2] + first_bias
    pre_first = pre_first.reshape(-1, HID)
    hidden_first = jnp.sin(first_omega * pre_first).astype(jnp.bfloat16)
    pre_hidden = jnp.dot(hidden_first, hidden_weight, preferred_element_type=jnp.float32) + hidden_bias
    hidden_second = jnp.sin(pre_hidden).astype(jnp.bfloat16)
    raw_kernel = jnp.dot(hidden_second, output_weight, preferred_element_type=jnp.float32) + output_bias
    kernel = (raw_kernel.reshape(NLAT, taps_lon, taps_lat, C) * tap_scale[..., None]).astype(jnp.bfloat16)
    flat_cot = cotangent.reshape(-1, C)
    mixed_cot = lax.dot_general(flat_cot, mix_weight, (((1,), (1,)), ((), ())), preferred_element_type=jnp.float32).astype(jnp.bfloat16).reshape(NLAT, NLON, C)
    row_pad = ((HLAT, HLAT), (0, 0), (0, 0))
    field_rows = jnp.pad(field, row_pad)
    cot_rows = jnp.pad(mixed_cot, row_pad)
    kernel_rows = jnp.pad(kernel, ((HLAT, HLAT), (0, 0), (0, 0), (0, 0)))
    cot_float = mixed_cot.astype(jnp.float32)

    def one_tap(carry, column):
        conv_total, back_total = carry
        offset = column - HLON
        field_moved = jnp.roll(field_rows, -offset, axis=1)
        cot_moved = jnp.roll(cot_rows, offset, axis=1)
        kernel_col = lax.dynamic_index_in_dim(kernel, column, 1, keepdims=False)
        kernel_ext = lax.dynamic_index_in_dim(kernel_rows, column, 1, keepdims=False)
        pieces = []
        for a in range(taps_lat):
            source = field_moved[a:a + NLAT].astype(jnp.float32)
            conv_total = conv_total + source * kernel_col[:, a][:, None, :].astype(jnp.float32)
            pieces.append(lax.optimization_barrier(jnp.sum(source * cot_float, axis=1)))
            row_from = 2 * HLAT - a
            back_total = back_total + cot_moved[row_from:row_from + NLAT].astype(jnp.float32) * kernel_ext[row_from:row_from + NLAT, a][:, None, :].astype(jnp.float32)
        return ((conv_total, back_total), jnp.stack(pieces, axis=1))
    zeros = jnp.zeros((NLAT, NLON, C), jnp.float32)
    (conv_total, back_total), tap_grads = lax.scan(one_tap, (zeros, zeros), jnp.arange(taps_lon))
    grad_kernel = jnp.transpose(tap_grads, (1, 0, 2, 3))
    conv_out = conv_total.astype(jnp.bfloat16)
    grad_field = back_total.astype(jnp.bfloat16)
    inverse = 1.0 / math.sqrt(NLAT * NLON)
    grad_mix = lax.dot_general(conv_out.reshape(-1, C), flat_cot, (((0,), (0,)), ((), ())), preferred_element_type=jnp.float32) * inverse
    grad_raw = (grad_kernel * tap_scale[..., None]).reshape(-1, C)
    grad_output_weight = jnp.dot(hidden_second.astype(jnp.float32).T, grad_raw, precision=highest) * inverse
    grad_output_bias = lax.optimization_barrier(jnp.sum(grad_raw, axis=0)) * inverse
    grad_pre_hidden = jnp.dot(grad_raw, output_weight.astype(jnp.float32).T, precision=highest) * jnp.cos(pre_hidden)
    grad_hidden_weight = jnp.dot(hidden_first.astype(jnp.float32).T, grad_pre_hidden, precision=highest) * inverse
    grad_hidden_bias = lax.optimization_barrier(jnp.sum(grad_pre_hidden, axis=0)) * inverse
    grad_pre_first = first_omega * jnp.dot(grad_pre_hidden, hidden_weight.astype(jnp.float32).T, precision=highest) * jnp.cos(first_omega * pre_first)
    features = jnp.stack((lon_coord.reshape(-1), lat_coord.reshape(-1), lat_sine.reshape(-1)), axis=0)
    grad_first_weight = jnp.dot(features, grad_pre_first, precision=highest) * inverse
    grad_first_bias = lax.optimization_barrier(jnp.sum(grad_pre_first, axis=0)) * inverse
    return (grad_field, grad_mix, grad_first_weight, grad_first_bias, grad_hidden_weight, grad_hidden_bias, grad_output_weight, grad_output_bias)
```

```python
import math

import jax
import jax.numpy as jnp
import numpy as np
from jax import lax
from jax.experimental import pallas as pl
from jax.experimental.pallas import tpu as pltpu
from jax.sharding import PartitionSpec as P

HLON = 32
HLAT = 4
NLAT = 32
NLON = 1024
ROWS = 4
COLS = 32
EXT = ROWS + 2 * HLAT
C = 256
HALF = 128
TAPS = 72
TLAT = 2 * HLAT + 1
GROUP = 4
SPAN = GROUP * TAPS
SLOTS = 56
OWN = ROWS * TLAT
WIN = 76
LINE = 104
PACK = 3 * C + HALF
MAGIC = 12582912.0
TURN = 1.0 / (2.0 * math.pi)

f32 = jnp.float32
bf16 = jnp.bfloat16

SIN_POLY = (0.99999995, -19.73917132, 64.93458165, -85.24010036, 56.24054044)
COS_POLY = (6.28318528, -41.34168067, 81.60248074, -76.58128456, 39.76072208)


def tables():
    out = np.zeros((4, 64), np.float32)
    width = np.arange(1, 64)
    out[0, 1:] = 1.0 / width
    out[1, :] = 1.0 / np.sqrt(2.0 * np.arange(64) + 1.0)
    out[2, :NLAT] = np.sin(np.pi * ((np.arange(NLAT) + 0.5) / NLAT - 0.5))
    return out


def horner(u, poly):
    total = poly[-1] * u + poly[-2]
    for c in poly[-3::-1]:
        total = total * u + c
    return total


def sine_cosine(turns):
    part = turns - ((turns + MAGIC) - MAGIC)
    h = jnp.abs(part) - 0.25
    u = h * h
    s = horner(u, SIN_POLY)
    return jnp.where(part < 0, -s, s), -h * horner(u, COS_POLY)


def reduce_eight(parts, masks):
    for shift, mask in zip((1, 2, 4), masks):
        merged = []
        for i in range(0, len(parts), 2):
            x, y = parts[i], parts[i + 1]
            merged.append(jnp.where(mask, x, y) + pltpu.roll(jnp.where(mask, y, x), 8 - shift, 0))
        parts = merged
    return parts[0]


def body(
    base_ref, lon_ref, lat_ref, tab_ref,
    field_ref, cot_ref, mix_ref, fw_ref, vec_ref, hw_ref, ow_ref,
    gfield_ref, pack_ref,
    slot_row, slot_tap, first_slot, low_tap, high_tap,
    line, fwin, mwin, kern, grad, sin_lon, cos_lon, sin_lat, cos_lat,
    h1_ref, h2_ref, c2_ref, conv, back, d_out, d_hid, d_small,
):
    base = base_ref[0]
    inverse = 1.0 / math.sqrt(NLAT * NLON)

    def grid_row(e):
        return base + e - HLAT

    def in_grid(e):
        i = grid_row(e)
        return jnp.logical_and(i >= 0, i < NLAT)

    def safe_row(e):
        return jnp.clip(grid_row(e), 0, NLAT - 1)

    def add_slots(e, lo, hi, count):
        low_tap[e] = lo
        high_tap[e] = hi
        first_slot[e] = count - lo

        def add(a, n):
            slot_row[n] = e
            slot_tap[n] = a
            return n + 1

        return lax.fori_loop(lo, hi + 1, add, count)

    def own_slots(r, count):
        e = r + HLAT
        i = grid_row(e)
        h = lat_ref[i]
        return add_slots(e, jnp.maximum(-h, -i), jnp.minimum(h, NLAT - 1 - i), count)

    own_count = lax.fori_loop(0, ROWS, own_slots, 0)

    def edge_slots(t, count):
        e = jnp.where(t < HLAT, t, t + ROWS)
        h = lat_ref[safe_row(e)]
        lo = jnp.maximum(-h, HLAT - e)
        hi = jnp.minimum(h, HLAT + ROWS - 1 - e)
        hi = jnp.where(in_grid(e), hi, lo - 1)
        return add_slots(e, lo, hi, count)

    slot_count = lax.fori_loop(0, 2 * HLAT, edge_slots, own_count)

    tap_index = lax.broadcasted_iota(jnp.int32, (TAPS, C), 0)
    lat_index = (lax.broadcasted_iota(jnp.int32, (16, C), 0) - HLAT).astype(f32)
    fw = fw_ref[...]
    vec = vec_ref[...]
    omega = 30.0 * TURN

    def angles(e, _):
        @pl.when(in_grid(e))
        def _():
            i = safe_row(e)
            w = lon_ref[i]
            lon = (tap_index - w).astype(f32) * tab_ref[0, w]
            phase = (lon * fw[0:1] + (tab_ref[2, i] * fw[2:3] + vec[0:1])) * omega
            s, c = sine_cosine(phase)
            sin_lon[e] = s
            cos_lon[e] = c
            s, c = sine_cosine((lat_index * tab_ref[0, lat_ref[i]]) * fw[1:2] * omega)
            sin_lat[e] = s
            cos_lat[e] = c

        return 0

    lax.fori_loop(0, EXT, angles, 0)

    def windows(source, target, front):
        def one(e, _):
            @pl.when(in_grid(e))
            def _():
                for h in range(2):
                    line[h, 0:8] = jnp.zeros((8, HALF), f32)
                    line[h, 96:LINE] = jnp.zeros((LINE - 96, HALF), f32)
                    line[h, front:front + 96] = source[e, :, h * HALF:(h + 1) * HALF].astype(f32)
                for h in range(2):
                    for p in range(WIN):
                        target[e, h, p] = line[h, pl.ds(p, 8, stride=4), :]

            return 0

        lax.fori_loop(0, EXT, one, 0)

    windows(field_ref, fwin, 0)
    windows(cot_ref, mwin, 8)

    def network(g, _):
        pos = [jnp.minimum(GROUP * g + q, slot_count - 1) for q in range(GROUP)]
        rows = [slot_row[n] for n in pos]
        hidden = []
        for n, e in zip(pos, rows):
            t = slot_tap[n] + HLAT
            hidden.append(sin_lon[e] * cos_lat[e, pl.ds(t, 1), :] + cos_lon[e] * sin_lat[e, pl.ds(t, 1), :])
        h1 = jnp.concatenate(hidden, axis=0).astype(bf16)
        pre = (jnp.dot(h1, hw_ref[...], preferred_element_type=f32) + vec[1:2]) * TURN
        s, c = sine_cosine(pre)
        h2 = s.astype(bf16)
        h1_ref[g] = h1
        h2_ref[g] = h2
        c2_ref[g] = c
        raw = jnp.dot(h2, ow_ref[...], preferred_element_type=f32) + vec[2:3]
        for q in range(GROUP):
            i = safe_row(rows[q])
            w = lon_ref[i]
            norm = tab_ref[1, w] * tab_ref[1, lat_ref[i]]
            k = jnp.where(tap_index <= 2 * w, raw[q * TAPS:(q + 1) * TAPS] * norm, 0.0)
            k = k.astype(bf16).astype(f32)
            at = pl.multiple_of((GROUP * g + q) * TAPS, 8)
            kern[0, pl.ds(at, TAPS), :] = k[:, :HALF]
            kern[1, pl.ds(at, TAPS), :] = k[:, HALF:]
        return 0

    lax.fori_loop(0, (slot_count + GROUP - 1) // GROUP, network, 0)

    sub = lax.broadcasted_iota(jnp.int32, (8, HALF), 0)
    masks = [(sub & bit) == 0 for bit in (1, 2, 4)]

    def conv_row(r, _):
        e = r + HLAT
        w = lon_ref[grid_row(e)]
        blocks = (2 * w + 8) // 8
        mine = [[mwin[e, h, HLON + 8 + t] for t in range(4)] for h in range(2)]

        def one_lat(a, total):
            slot = first_slot[e] + a

            def one_block(b, total):
                new = []
                start = HLON - w + 8 * b
                at = slot * TAPS + 8 * b
                for h in range(2):
                    acc = list(total[4 * h:4 * h + 4])
                    parts = []
                    x = [fwin[e + a, h, start + t] for t in range(11)]
                    for k in range(8):
                        kv = kern[h, pl.ds(at + k, 8, stride=0), :]
                        for t in range(4):
                            acc[t] = acc[t] + x[k + t] * kv
                        p = [x[k + t] * mine[h][t] for t in range(4)]
                        parts.append((p[0] + p[1]) + (p[2] + p[3]))
                    grad[h, pl.ds(pl.multiple_of(at, 8), 8), :] = reduce_eight(parts, masks)
                    new += acc
                return tuple(new)

            return lax.fori_loop(0, blocks, one_block, total)

        zero = jnp.zeros((8, HALF), f32)
        total = lax.fori_loop(low_tap[e], high_tap[e] + 1, one_lat, (zero,) * 8)
        for h in range(2):
            for t in range(4):
                conv[h, pl.ds(r * COLS + t, 8, stride=4), :] = total[4 * h + t]
        return 0

    lax.fori_loop(0, ROWS, conv_row, 0)

    def back_row(r, _):
        def one_source(e, total):
            a = r + HLAT - e
            i = safe_row(e)
            w = lon_ref[i]
            live = jnp.logical_and(in_grid(e), jnp.abs(a) <= lat_ref[i])
            blocks = jnp.where(live, (2 * w + 8) // 8, 0)
            slot = first_slot[e] + a

            def one_block(b, total):
                new = []
                start = HLON + 1 + w - 8 * b
                at = slot * TAPS + 8 * b
                for h in range(2):
                    acc = list(total[4 * h:4 * h + 4])
                    x = [mwin[e, h, start + t] for t in range(11)]
                    for k in range(8):
                        kv = kern[h, pl.ds(at + k, 8, stride=0), :]
                        for t in range(4):
                            acc[t] = acc[t] + x[7 - k + t] * kv
                    new += acc
                return tuple(new)

            return lax.fori_loop(0, blocks, one_block, total)

        zero = jnp.zeros((8, HALF), f32)
        total = lax.fori_loop(r, r + TLAT, one_source, (zero,) * 8)
        for h in range(2):
            for t in range(4):
                back[h, pl.ds(r * COLS + t, 8, stride=4), :] = total[4 * h + t]
        return 0

    lax.fori_loop(0, ROWS, back_row, 0)
    for h in range(2):
        gfield_ref[:, h * HALF:(h + 1) * HALF] = back[h].astype(bf16)
        got = lax.dot_general(
            conv[h].astype(bf16), mix_ref[...], (((0,), (0,)), ((), ())), preferred_element_type=f32
        )
        pack_ref[h * HALF:(h + 1) * HALF, 0:C] = (got * inverse).astype(bf16)

    d_out[...] = jnp.zeros_like(d_out)
    d_hid[...] = jnp.zeros_like(d_hid)
    d_small[...] = jnp.zeros_like(d_small)

    def adjoint(g, _):
        raw = []
        pos = [jnp.minimum(GROUP * g + q, own_count - 1) for q in range(GROUP)]
        rows = [slot_row[n] for n in pos]
        for q in range(GROUP):
            i = grid_row(rows[q])
            w = lon_ref[i]
            norm = tab_ref[1, w] * tab_ref[1, lat_ref[i]]
            limit = jnp.where(GROUP * g + q < own_count, 2 * w, -1)
            at = pl.multiple_of(pos[q] * TAPS, 8)
            part = jnp.concatenate([grad[0, pl.ds(at, TAPS), :], grad[1, pl.ds(at, TAPS), :]], axis=1)
            raw.append(jnp.where(tap_index <= limit, part * norm, 0.0))
        raw = jnp.concatenate(raw, axis=0)
        raw_low = raw.astype(bf16)
        h1 = h1_ref[g]
        h2 = h2_ref[g]
        rows_by_rows = (((0,), (0,)), ((), ()))
        d_out[...] += lax.dot_general(h2, raw_low, rows_by_rows, preferred_element_type=f32)
        d_small[5:6, :] += jnp.sum(raw, axis=0, keepdims=True)
        gp = lax.dot_general(
            raw_low, ow_ref[...], (((1,), (1,)), ((), ())), preferred_element_type=f32
        ) * c2_ref[g]
        gp_low = gp.astype(bf16)
        d_hid[...] += lax.dot_general(h1, gp_low, rows_by_rows, preferred_element_type=f32)
        d_small[4:5, :] += jnp.sum(gp, axis=0, keepdims=True)
        gf = lax.dot_general(
            gp_low, hw_ref[...], (((1,), (1,)), ((), ())), preferred_element_type=f32
        )
        for q in range(GROUP):
            e = rows[q]
            i = grid_row(e)
            w = lon_ref[i]
            a = slot_tap[pos[q]]
            t = a + HLAT
            c1 = cos_lon[e] * cos_lat[e, pl.ds(t, 1), :] - sin_lon[e] * sin_lat[e, pl.ds(t, 1), :]
            gq = gf[q * TAPS:(q + 1) * TAPS] * c1
            lon = (tap_index - w).astype(f32) * tab_ref[0, w]
            total = jnp.sum(gq, axis=0, keepdims=True)
            d_small[0:1, :] += jnp.sum(gq * lon, axis=0, keepdims=True)
            d_small[1:2, :] += total * (a.astype(f32) * tab_ref[0, lat_ref[i]])
            d_small[2:3, :] += total * tab_ref[2, i]
            d_small[3:4, :] += total
        return 0

    lax.fori_loop(0, (own_count + GROUP - 1) // GROUP, adjoint, 0)
    pack_ref[:, C:2 * C] = (d_hid[...] * inverse).astype(bf16)
    pack_ref[:, 2 * C:3 * C] = (d_out[...] * inverse).astype(bf16)
    d_small[0:4, :] = d_small[0:4, :] * 30.0
    pack_ref[:, 3 * C:] = jnp.transpose(d_small[...] * inverse).astype(bf16)


def local_pass(base, lon_half, lat_half, field, cot_mixed, cotangent, fw, vec, hw, ow):
    smem = pl.BlockSpec(memory_space=pltpu.SMEM)
    vmem = pl.BlockSpec(memory_space=pltpu.VMEM)
    groups = SLOTS // GROUP
    return pl.pallas_call(
        body,
        out_shape=(
            jax.ShapeDtypeStruct((ROWS * COLS, C), bf16),
            jax.ShapeDtypeStruct((C, PACK), bf16),
        ),
        in_specs=[smem] * 4 + [vmem] * 7,
        out_specs=(vmem, vmem),
        scratch_shapes=[
            pltpu.SMEM((SLOTS + 8,), jnp.int32),
            pltpu.SMEM((SLOTS + 8,), jnp.int32),
            pltpu.SMEM((16,), jnp.int32),
            pltpu.SMEM((16,), jnp.int32),
            pltpu.SMEM((16,), jnp.int32),
            pltpu.VMEM((2, LINE, HALF), f32),
            pltpu.VMEM((EXT, 2, WIN, 8, HALF), f32),
            pltpu.VMEM((EXT, 2, WIN, 8, HALF), f32),
            pltpu.VMEM((2, SLOTS * TAPS, HALF), f32),
            pltpu.VMEM((2, OWN * TAPS, HALF), f32),
            pltpu.VMEM((EXT, TAPS, C), f32),
            pltpu.VMEM((EXT, TAPS, C), f32),
            pltpu.VMEM((EXT, 16, C), f32),
            pltpu.VMEM((EXT, 16, C), f32),
            pltpu.VMEM((groups, SPAN, C), bf16),
            pltpu.VMEM((groups, SPAN, C), bf16),
            pltpu.VMEM((groups, SPAN, C), f32),
            pltpu.VMEM((2, ROWS * COLS, HALF), f32),
            pltpu.VMEM((2, ROWS * COLS, HALF), f32),
            pltpu.VMEM((C, C), f32),
            pltpu.VMEM((C, C), f32),
            pltpu.VMEM((HALF, C), f32),
        ],
        compiler_params=pltpu.CompilerParams(vmem_limit_bytes=56 * 1024 * 1024),
        name="local_pass",
    )(base, lon_half, lat_half, jnp.asarray(tables()), field, cot_mixed, cotangent, fw, vec, hw, ow)


def extended(block, axis, dim, width, periodic):
    count = lax.axis_size(axis)
    forward = [(i, i + 1) for i in range(count - 1)]
    if periodic:
        forward.append((count - 1, 0))
    backward = [(target, source) for source, target in forward]
    low = lax.ppermute(lax.slice_in_dim(block, block.shape[dim] - width, None, axis=dim), axis, forward)
    high = lax.ppermute(lax.slice_in_dim(block, 0, width, axis=dim), axis, backward)
    return jnp.concatenate([low, block, high], axis=dim)


def spread(block, axis):
    return lax.all_to_all(block, axis, 0, 0, tiled=True)


def total_of(pack):
    rows, width = pack.shape
    lat, lon = lax.axis_size("lat"), lax.axis_size("lon")
    part = spread(pack.reshape(lat, rows // lat, width), "lat")
    part = jnp.sum(part.astype(f32), axis=0).astype(bf16)
    line = spread(part, "lon")
    line = jnp.sum(line.astype(f32), axis=0, keepdims=True).astype(bf16)
    part = spread(jnp.broadcast_to(line, (lon, width)), "lon")
    full = spread(jnp.broadcast_to(part[None], (lat, lon, width)), "lat")
    return full.reshape(rows, width)


def shards(
    field, cotangent, mix_weight, first_weight, first_bias, hidden_weight, hidden_bias,
    output_weight, output_bias, lon_half, lat_half,
):
    flat_cot = cotangent.reshape(-1, C)
    mixed = lax.dot_general(
        flat_cot, mix_weight, (((1,), (1,)), ((), ())), preferred_element_type=f32
    ).astype(bf16).reshape(ROWS, COLS, C)
    both = jnp.stack((field, mixed), axis=0)
    both = extended(both, "lat", 1, HLAT, False)
    both = extended(both, "lon", 2, HLON, True)
    base = (lax.axis_index("lat") * ROWS).astype(jnp.int32).reshape(1)
    vec = jnp.stack((first_bias, hidden_bias, output_bias), axis=0)
    grad_field, pack = local_pass(
        base, lon_half, lat_half, both[0], both[1], flat_cot, first_weight, vec,
        hidden_weight, output_weight,
    )
    summed = total_of(pack).astype(f32)
    small = summed[:, 3 * C:3 * C + 8].T
    return (
        grad_field.reshape(ROWS, COLS, C),
        summed[:, :C],
        small[0:3],
        small[3],
        summed[:, C:2 * C],
        small[4],
        summed[:, 2 * C:3 * C],
        small[5],
    )


def solution(mesh):
    in_specs = (P("lat", "lon", None), P("lat", "lon", None)) + (P(),) * 9
    out_specs = (P("lat", "lon", None),) + (P(),) * 7
    return jax.shard_map(shards, mesh=mesh, in_specs=in_specs, out_specs=out_specs, check_vma=False)
```

```python
import math

import jax
import jax.numpy as jnp
import numpy as np
from jax import lax
from jax.experimental import pallas as pl
from jax.experimental.pallas import tpu as pltpu
from jax.sharding import Mesh
from jax.sharding import PartitionSpec as P

HLON = 32
HLAT = 4
NLAT = 32
NLON = 1024
ROWS = 4
COLS = 32
EXT = ROWS + 2 * HLAT
C = 256
HALF = 128
TAPS = 72
TLAT = 2 * HLAT + 1
GROUP = 4
SPAN = GROUP * TAPS
SLOTS = 56
OWN = ROWS * TLAT
WIN = 76
LINE = 104
PACK = 3 * C + HALF
MAGIC = 12582912.0
TURN = 1.0 / (2.0 * math.pi)

f32 = jnp.float32
bf16 = jnp.bfloat16

SIN_POLY = (0.99999995, -19.73917132, 64.93458165, -85.24010036, 56.24054044)
COS_POLY = (6.28318528, -41.34168067, 81.60248074, -76.58128456, 39.76072208)


def tables():
    out = np.zeros((4, 64), np.float32)
    width = np.arange(1, 64)
    out[0, 1:] = 1.0 / width
    out[1, :] = 1.0 / np.sqrt(2.0 * np.arange(64) + 1.0)
    out[2, :NLAT] = np.sin(np.pi * ((np.arange(NLAT) + 0.5) / NLAT - 0.5))
    return out


def horner(u, poly):
    total = poly[-1] * u + poly[-2]
    for c in poly[-3::-1]:
        total = total * u + c
    return total


def sine_cosine(turns):
    part = turns - ((turns + MAGIC) - MAGIC)
    h = jnp.abs(part) - 0.25
    u = h * h
    s = horner(u, SIN_POLY)
    return jnp.where(part < 0, -s, s), -h * horner(u, COS_POLY)


def reduce_eight(parts, masks):
    for shift, mask in zip((1, 2, 4), masks):
        merged = []
        for i in range(0, len(parts), 2):
            x, y = parts[i], parts[i + 1]
            merged.append(jnp.where(mask, x, y) + pltpu.roll(jnp.where(mask, y, x), 8 - shift, 0))
        parts = merged
    return parts[0]


def grid_row(place_ref, e):
    return place_ref[0] + e - HLAT


def in_grid(place_ref, e):
    i = grid_row(place_ref, e)
    return jnp.logical_and(i >= 0, i < NLAT)


def safe_row(place_ref, e):
    return jnp.clip(grid_row(place_ref, e), 0, NLAT - 1)


def number_slots(place_ref, lat_ref, slot_row, slot_tap, first_slot, low_tap, high_tap):
    def add_slots(e, lo, hi, count):
        low_tap[e] = lo
        high_tap[e] = hi
        first_slot[e] = count - lo

        def add(a, n):
            slot_row[n] = e
            slot_tap[n] = a
            return n + 1

        return lax.fori_loop(lo, hi + 1, add, count)

    def own_slots(r, count):
        e = r + HLAT
        i = grid_row(place_ref, e)
        h = lat_ref[i]
        return add_slots(e, jnp.maximum(-h, -i), jnp.minimum(h, NLAT - 1 - i), count)

    own_count = lax.fori_loop(0, ROWS, own_slots, 0)

    def edge_slots(t, count):
        e = jnp.where(t < HLAT, t, t + ROWS)
        h = lat_ref[safe_row(place_ref, e)]
        lo = jnp.maximum(-h, HLAT - e)
        hi = jnp.minimum(h, HLAT + ROWS - 1 - e)
        hi = jnp.where(in_grid(place_ref, e), hi, lo - 1)
        return add_slots(e, lo, hi, count)

    return own_count, lax.fori_loop(0, 2 * HLAT, edge_slots, own_count)


def network_body(
    place_ref, lon_ref, lat_ref, tab_ref, fw_ref, vec_ref, hw_ref, ow_ref,
    kern, h1_ref, h2_ref, c2_ref, own_sin_lon, own_cos_lon, own_sin_lat, own_cos_lat,
    slot_row, slot_tap, first_slot, low_tap, high_tap, sin_lon, cos_lon, sin_lat, cos_lat,
):
    own_count, slot_count = number_slots(place_ref, lat_ref, slot_row, slot_tap, first_slot, low_tap, high_tap)
    own_groups = (own_count + GROUP - 1) // GROUP
    tap_index = lax.broadcasted_iota(jnp.int32, (TAPS, C), 0)
    lat_index = (lax.broadcasted_iota(jnp.int32, (16, C), 0) - HLAT).astype(f32)
    fw = fw_ref[...]
    vec = vec_ref[...]
    omega = 30.0 * TURN

    def angles(e, _):
        @pl.when(in_grid(place_ref, e))
        def _():
            i = safe_row(place_ref, e)
            w = lon_ref[i]
            lon = (tap_index - w).astype(f32) * tab_ref[0, w]
            phase = (lon * fw[0:1] + (tab_ref[2, i] * fw[2:3] + vec[0:1])) * omega
            s, c = sine_cosine(phase)
            sin_lon[e] = s
            cos_lon[e] = c
            s, c = sine_cosine((lat_index * tab_ref[0, lat_ref[i]]) * fw[1:2] * omega)
            sin_lat[e] = s
            cos_lat[e] = c

        return 0

    lax.fori_loop(0, EXT, angles, 0)

    def network(g, _):
        pos = [jnp.minimum(GROUP * g + q, slot_count - 1) for q in range(GROUP)]
        rows = [slot_row[n] for n in pos]
        hidden = []
        for n, e in zip(pos, rows):
            t = slot_tap[n] + HLAT
            hidden.append(sin_lon[e] * cos_lat[e, pl.ds(t, 1), :] + cos_lon[e] * sin_lat[e, pl.ds(t, 1), :])
        h1 = jnp.concatenate(hidden, axis=0).astype(bf16)
        pre = (jnp.dot(h1, hw_ref[...], preferred_element_type=f32) + vec[1:2]) * TURN
        s, c = sine_cosine(pre)
        h2 = s.astype(bf16)

        @pl.when(g < own_groups)
        def _():
            h1_ref[g] = h1
            h2_ref[g] = h2
            c2_ref[g] = c

        raw = jnp.dot(h2, ow_ref[...], preferred_element_type=f32) + vec[2:3]
        for q in range(GROUP):
            i = safe_row(place_ref, rows[q])
            w = lon_ref[i]
            norm = tab_ref[1, w] * tab_ref[1, lat_ref[i]]
            k = jnp.where(tap_index <= 2 * w, raw[q * TAPS:(q + 1) * TAPS] * norm, 0.0)
            k = k.astype(bf16).astype(f32)
            at = pl.multiple_of((GROUP * g + q) * TAPS, 8)
            kern[0, pl.ds(at, TAPS), :] = k[:, :HALF]
            kern[1, pl.ds(at, TAPS), :] = k[:, HALF:]
        return 0

    lax.fori_loop(0, (slot_count + GROUP - 1) // GROUP, network, 0)
    for own, every in (
        (own_sin_lon, sin_lon), (own_cos_lon, cos_lon), (own_sin_lat, sin_lat), (own_cos_lat, cos_lat),
    ):
        own[...] = every[HLAT:HLAT + ROWS]


def network_pass(place, lon_half, lat_half, fw, vec, hw, ow):
    smem = pl.BlockSpec(memory_space=pltpu.SMEM)
    vmem = pl.BlockSpec(memory_space=pltpu.VMEM)
    return pl.pallas_call(
        network_body,
        out_shape=(
            jax.ShapeDtypeStruct((2, SLOTS * TAPS, HALF), f32),
            jax.ShapeDtypeStruct((OWN // GROUP, SPAN, C), bf16),
            jax.ShapeDtypeStruct((OWN // GROUP, SPAN, C), bf16),
            jax.ShapeDtypeStruct((OWN // GROUP, SPAN, C), f32),
            jax.ShapeDtypeStruct((ROWS, TAPS, C), f32),
            jax.ShapeDtypeStruct((ROWS, TAPS, C), f32),
            jax.ShapeDtypeStruct((ROWS, 16, C), f32),
            jax.ShapeDtypeStruct((ROWS, 16, C), f32),
        ),
        in_specs=[smem] * 4 + [vmem] * 4,
        out_specs=(vmem,) * 8,
        scratch_shapes=[
            pltpu.SMEM((SLOTS + 8,), jnp.int32),
            pltpu.SMEM((SLOTS + 8,), jnp.int32),
            pltpu.SMEM((16,), jnp.int32),
            pltpu.SMEM((16,), jnp.int32),
            pltpu.SMEM((16,), jnp.int32),
            pltpu.VMEM((EXT, TAPS, C), f32),
            pltpu.VMEM((EXT, TAPS, C), f32),
            pltpu.VMEM((EXT, 16, C), f32),
            pltpu.VMEM((EXT, 16, C), f32),
        ],
        compiler_params=pltpu.CompilerParams(vmem_limit_bytes=22 * 1024 * 1024),
        cost_estimate=pl.CostEstimate(flops=6_000_000_000, bytes_accessed=16_000_000, transcendentals=0),
        name="network_pass",
    )(place, lon_half, lat_half, jnp.asarray(tables()), fw, vec, hw, ow)


def body(
    place_ref, lon_ref, lat_ref, tab_ref,
    here_ref, inner_ref, outer_ref, cot_ref, hw_ref, ow_ref,
    kern, h1_ref, h2_ref, c2_ref, sin_lon, cos_lon, sin_lat, cos_lat,
    gfield_ref, keep_ref, send_ref,
    slot_row, slot_tap, first_slot, low_tap, high_tap,
    line, fwin, mwin, grad, conv, back, d_mix, d_out, d_hid, d_small, d_side,
):
    inverse = 1.0 / math.sqrt(NLAT * NLON)
    own_count, slot_count = number_slots(place_ref, lat_ref, slot_row, slot_tap, first_slot, low_tap, high_tap)
    tap_index = lax.broadcasted_iota(jnp.int32, (TAPS, C), 0)
    lat_odd = place_ref[2]
    core = place_ref[1]
    left_inner = core == 1

    def windows(which, target, front):
        def one(e, _):
            @pl.when(in_grid(place_ref, e))
            def _():
                band = e // ROWS
                part = jnp.where(band == 1, 0, jnp.where((band == 2) == (lat_odd == 1), 2, 1))
                row = e % ROWS
                for h in range(2):
                    lanes = slice(h * HALF, (h + 1) * HALF)
                    near = inner_ref[part, which, row, :, lanes].astype(f32)
                    far = outer_ref[part, which, row, :, lanes].astype(f32)
                    line[h, 0:8] = jnp.zeros((8, HALF), f32)
                    line[h, 96:LINE] = jnp.zeros((LINE - 96, HALF), f32)
                    line[h, front:front + 32] = jnp.where(left_inner, near, far)
                    line[h, front + 32:front + 64] = here_ref[part, which, row, :, lanes].astype(f32)
                    line[h, front + 64:front + 96] = jnp.where(left_inner, far, near)
                for h in range(2):
                    for p in range(WIN):
                        target[e, h, p] = line[h, pl.ds(p, 8, stride=4), :]

            return 0

        lax.fori_loop(0, EXT, one, 0)

    windows(0, fwin, 0)
    windows(1, mwin, 8)

    sub = lax.broadcasted_iota(jnp.int32, (8, HALF), 0)
    masks = [(sub & bit) == 0 for bit in (1, 2, 4)]

    def conv_row(r, _):
        e = r + HLAT
        w = lon_ref[grid_row(place_ref, e)]
        blocks = (2 * w + 8) // 8
        mine = [[mwin[e, h, HLON + 8 + t] for t in range(4)] for h in range(2)]

        def one_lat(a, total):
            slot = first_slot[e] + a

            def one_block(b, total):
                new = []
                start = HLON - w + 8 * b
                at = slot * TAPS + 8 * b
                for h in range(2):
                    acc = list(total[4 * h:4 * h + 4])
                    parts = []
                    x = [fwin[e + a, h, start + t] for t in range(11)]
                    for k in range(8):
                        kv = kern[h, pl.ds(at + k, 8, stride=0), :]
                        for t in range(4):
                            acc[t] = acc[t] + x[k + t] * kv
                        p = [x[k + t] * mine[h][t] for t in range(4)]
                        parts.append((p[0] + p[1]) + (p[2] + p[3]))
                    grad[h, pl.ds(pl.multiple_of(at, 8), 8), :] = reduce_eight(parts, masks)
                    new += acc
                return tuple(new)

            return lax.fori_loop(0, blocks, one_block, total)

        zero = jnp.zeros((8, HALF), f32)
        total = lax.fori_loop(low_tap[e], high_tap[e] + 1, one_lat, (zero,) * 8)
        for h in range(2):
            for t in range(4):
                conv[h, pl.ds(r * COLS + t, 8, stride=4), :] = total[4 * h + t]
        return 0

    lax.fori_loop(0, ROWS, conv_row, 0)

    def back_row(r, _):
        def one_source(e, total):
            a = r + HLAT - e
            i = safe_row(place_ref, e)
            w = lon_ref[i]
            live = jnp.logical_and(in_grid(place_ref, e), jnp.abs(a) <= lat_ref[i])
            blocks = jnp.where(live, (2 * w + 8) // 8, 0)
            slot = first_slot[e] + a

            def one_block(b, total):
                new = []
                start = HLON + 1 + w - 8 * b
                at = slot * TAPS + 8 * b
                for h in range(2):
                    acc = list(total[4 * h:4 * h + 4])
                    x = [mwin[e, h, start + t] for t in range(11)]
                    for k in range(8):
                        kv = kern[h, pl.ds(at + k, 8, stride=0), :]
                        for t in range(4):
                            acc[t] = acc[t] + x[7 - k + t] * kv
                    new += acc
                return tuple(new)

            return lax.fori_loop(0, blocks, one_block, total)

        zero = jnp.zeros((8, HALF), f32)
        total = lax.fori_loop(r, r + TLAT, one_source, (zero,) * 8)
        for h in range(2):
            for t in range(4):
                back[h, pl.ds(r * COLS + t, 8, stride=4), :] = total[4 * h + t]
        return 0

    lax.fori_loop(0, ROWS, back_row, 0)
    for h in range(2):
        gfield_ref[:, h * HALF:(h + 1) * HALF] = back[h].astype(bf16)
        got = lax.dot_general(
            conv[h].astype(bf16), cot_ref[...], (((0,), (0,)), ((), ())), preferred_element_type=f32
        )
        d_mix[h * HALF:(h + 1) * HALF, :] = got

    d_out[...] = jnp.zeros_like(d_out)
    d_hid[...] = jnp.zeros_like(d_hid)
    d_small[...] = jnp.zeros_like(d_small)

    def adjoint(g, _):
        raw = []
        pos = [jnp.minimum(GROUP * g + q, own_count - 1) for q in range(GROUP)]
        rows = [slot_row[n] for n in pos]
        for q in range(GROUP):
            i = grid_row(place_ref, rows[q])
            w = lon_ref[i]
            norm = tab_ref[1, w] * tab_ref[1, lat_ref[i]]
            limit = jnp.where(GROUP * g + q < own_count, 2 * w, -1)
            at = pl.multiple_of(pos[q] * TAPS, 8)
            part = jnp.concatenate([grad[0, pl.ds(at, TAPS), :], grad[1, pl.ds(at, TAPS), :]], axis=1)
            raw.append(jnp.where(tap_index <= limit, part * norm, 0.0))
        raw = jnp.concatenate(raw, axis=0)
        raw_low = raw.astype(bf16)
        h1 = h1_ref[g]
        h2 = h2_ref[g]
        rows_by_rows = (((0,), (0,)), ((), ()))
        d_out[...] += lax.dot_general(h2, raw_low, rows_by_rows, preferred_element_type=f32)
        d_small[5:6, :] += jnp.sum(raw, axis=0, keepdims=True)
        gp = lax.dot_general(
            raw_low, ow_ref[...], (((1,), (1,)), ((), ())), preferred_element_type=f32
        ) * c2_ref[g]
        gp_low = gp.astype(bf16)
        d_hid[...] += lax.dot_general(h1, gp_low, rows_by_rows, preferred_element_type=f32)
        d_small[4:5, :] += jnp.sum(gp, axis=0, keepdims=True)
        gf = lax.dot_general(
            gp_low, hw_ref[...], (((1,), (1,)), ((), ())), preferred_element_type=f32
        )
        for q in range(GROUP):
            e = rows[q]
            i = grid_row(place_ref, e)
            w = lon_ref[i]
            a = slot_tap[pos[q]]
            t = a + HLAT
            c1 = cos_lon[e - HLAT] * cos_lat[e - HLAT, pl.ds(t, 1), :] - sin_lon[e - HLAT] * sin_lat[e - HLAT, pl.ds(t, 1), :]
            gq = gf[q * TAPS:(q + 1) * TAPS] * c1
            lon = (tap_index - w).astype(f32) * tab_ref[0, w]
            total = jnp.sum(gq, axis=0, keepdims=True)
            d_small[0:1, :] += jnp.sum(gq * lon, axis=0, keepdims=True)
            d_small[1:2, :] += total * (a.astype(f32) * tab_ref[0, lat_ref[i]])
            d_small[2:3, :] += total * tab_ref[2, i]
            d_small[3:4, :] += total
        return 0

    lax.fori_loop(0, (own_count + GROUP - 1) // GROUP, adjoint, 0)
    d_small[0:4, :] = d_small[0:4, :] * 30.0
    d_side[...] = jnp.transpose(d_small[...])
    for target, half in ((keep_ref, core), (send_ref, 1 - core)):
        rows = pl.ds(pl.multiple_of(half * HALF, HALF), HALF)
        for q, source in enumerate((d_mix, d_hid, d_out, d_side)):
            part = source[rows, :] * inverse
            target[:, q * C:q * C + part.shape[1]] = part.astype(bf16)


def unpack_body(place_ref, own_ref, other_ref, mix_ref, hid_ref, out_ref, first_ref, fb_ref, hb_ref, ob_ref, side):
    core = place_ref[1]
    for source, half in ((own_ref, core), (other_ref, 1 - core)):
        rows = pl.ds(pl.multiple_of(half * HALF, HALF), HALF)
        for q, target in enumerate((mix_ref, hid_ref, out_ref)):
            target[rows, :] = source[:, q * C:(q + 1) * C].astype(f32)
        side[rows, :] = source[:, 3 * C:].astype(f32)
    small = jnp.transpose(side[...])
    first_ref[...] = small[0:3]
    fb_ref[...] = small[3:4]
    hb_ref[...] = small[4:5]
    ob_ref[...] = small[5:6]


def unpack(place, own, other):
    vmem = pl.BlockSpec(memory_space=pltpu.VMEM)
    square = jax.ShapeDtypeStruct((C, C), f32)
    line = jax.ShapeDtypeStruct((1, C), f32)
    return pl.pallas_call(
        unpack_body,
        out_shape=(square, square, square, jax.ShapeDtypeStruct((3, C), f32), line, line, line),
        in_specs=[pl.BlockSpec(memory_space=pltpu.SMEM)] + [vmem] * 2,
        out_specs=(vmem,) * 7,
        scratch_shapes=[pltpu.VMEM((C, HALF), f32)],
        compiler_params=pltpu.CompilerParams(vmem_limit_bytes=8 * 1024 * 1024),
        name="unpack",
    )(place, own, other)


def local_pass(place, lon_half, lat_half, here, inner, outer, cotangent, hw, ow, saved):
    smem = pl.BlockSpec(memory_space=pltpu.SMEM)
    vmem = pl.BlockSpec(memory_space=pltpu.VMEM)
    return pl.pallas_call(
        body,
        out_shape=(
            jax.ShapeDtypeStruct((ROWS * COLS, C), bf16),
            jax.ShapeDtypeStruct((C // 2, PACK), bf16),
            jax.ShapeDtypeStruct((C // 2, PACK), bf16),
        ),
        in_specs=[smem] * 4 + [vmem] * 14,
        out_specs=(vmem,) * 3,
        scratch_shapes=[
            pltpu.SMEM((SLOTS + 8,), jnp.int32),
            pltpu.SMEM((SLOTS + 8,), jnp.int32),
            pltpu.SMEM((16,), jnp.int32),
            pltpu.SMEM((16,), jnp.int32),
            pltpu.SMEM((16,), jnp.int32),
            pltpu.VMEM((2, LINE, HALF), f32),
            pltpu.VMEM((EXT, 2, WIN, 8, HALF), f32),
            pltpu.VMEM((EXT, 2, WIN, 8, HALF), f32),
            pltpu.VMEM((2, OWN * TAPS, HALF), f32),
            pltpu.VMEM((2, ROWS * COLS, HALF), f32),
            pltpu.VMEM((2, ROWS * COLS, HALF), f32),
            pltpu.VMEM((C, C), f32),
            pltpu.VMEM((C, C), f32),
            pltpu.VMEM((C, C), f32),
            pltpu.VMEM((HALF, C), f32),
            pltpu.VMEM((C, HALF), f32),
        ],
        compiler_params=pltpu.CompilerParams(vmem_limit_bytes=40 * 1024 * 1024),
        cost_estimate=pl.CostEstimate(flops=9_000_000_000, bytes_accessed=24_000_000, transcendentals=0),
        name="local_pass",
    )(place, lon_half, lat_half, jnp.asarray(tables()), here, inner, outer, cotangent, hw, ow, *saved)


def swap(block, axis, pairs):
    return lax.ppermute(block, axis, pairs)


LAT_INNER = [(i, i ^ 1) for i in range(8)]
LAT_OUTER = [(i, i + 1 if i % 2 else i - 1) for i in range(1, 7)]
LON_INNER = [(i, i ^ 1) for i in range(32)]
LON_OUTER = [(i, (i + 1 if i % 2 else i - 1) % 32) for i in range(32)]
PLANE = ("y", "x_low", "x_high")


def spread(block, axis):
    return lax.all_to_all(block, axis, 0, 0, tiled=True)


def total_of(place, keep, send):
    total = (keep.astype(f32) + swap(send, "core", [(0, 1), (1, 0)]).astype(f32)).astype(bf16)
    total = spread(total.reshape(16, 8, PACK), PLANE)
    total = jnp.sum(total.astype(f32), axis=0)
    for bits in (1, 2, 6):
        total = total + swap(total, "z", [(i, i ^ bits) for i in range(8)])
    own = spread(jnp.broadcast_to(total.astype(bf16)[None], (16, 8, PACK)), PLANE).reshape(HALF, PACK)
    return unpack(place, own, swap(own, "core", [(0, 1), (1, 0)]))


LAT = ("y", "x_low")
LON = ("z", "x_high", "core")


def shards(
    field, cotangent, mix_weight, first_weight, first_bias, hidden_weight, hidden_bias,
    output_weight, output_bias, lon_half, lat_half,
):
    flat_cot = cotangent.reshape(-1, C)
    mixed = lax.dot_general(
        flat_cot, mix_weight, (((1,), (1,)), ((), ())), preferred_element_type=f32
    ).astype(bf16).reshape(ROWS, COLS, C)
    both = jnp.stack((field, mixed), axis=0)
    here = jnp.stack((both, swap(both, LAT, LAT_INNER), swap(both, LAT, LAT_OUTER)), axis=0)
    inner = swap(here, LON, LON_INNER)
    outer = swap(here, LON, LON_OUTER)
    lat = lax.axis_index("y") * 2 + lax.axis_index("x_low")
    place = jnp.stack((lat * ROWS, lax.axis_index("core"), lat % 2)).astype(jnp.int32)
    vec = jnp.stack((first_bias, hidden_bias, output_bias), axis=0)
    saved = network_pass(place, lon_half, lat_half, first_weight, vec, hidden_weight, output_weight)
    grad_field, keep, send = local_pass(
        place, lon_half, lat_half, here, inner, outer, flat_cot, hidden_weight, output_weight, saved,
    )
    mix, hid, out, first, fb, hb, ob = total_of(place, keep, send)
    return (
        grad_field.reshape(ROWS, COLS, C), mix, first, fb.reshape(C), hid, hb.reshape(C), out, ob.reshape(C),
    )


def solution(mesh):
    split = Mesh(mesh.devices.reshape(8, 2, 2, 4, 2), ("z", "x_high", "core", "y", "x_low"))
    grid = P(LAT, LON, None)
    in_specs = (grid, grid) + (P(),) * 9
    out_specs = (grid,) + (P(),) * 7
    return jax.shard_map(shards, mesh=split, in_specs=in_specs, out_specs=out_specs, check_vma=False)
```

```python
import functools
import math

import jax
import jax.numpy as jnp
import numpy as np
from jax import lax
from jax.experimental import pallas as pl
from jax.experimental.pallas import tpu as pltpu
from jax.sharding import Mesh
from jax.sharding import PartitionSpec as P

HLON = 32
HLAT = 4
NLAT = 32
NLON = 1024
ROWS = 4
COLS = 32
EXT = ROWS + 2 * HLAT
C = 256
HALF = 128
TAPS = 72
TLAT = 2 * HLAT + 1
GROUP = 4
SPAN = GROUP * TAPS
SLOTS = 56
OWN = ROWS * TLAT
WIN = 76
PAIRS = 40
HEAD = 3
LINE = 104
PACK = 3 * C + HALF
MAGIC = 12582912.0
TURN = 1.0 / (2.0 * math.pi)

f32 = jnp.float32
bf16 = jnp.bfloat16

SIN_POLY = (0.99999995, -19.73917132, 64.93458165, -85.24010036, 56.24054044)
COS_POLY = (6.28318528, -41.34168067, 81.60248074, -76.58128456, 39.76072208)


def tables(lon_half, lat_half):
    lon, lat = lon_half.astype(f32), lat_half.astype(f32)
    sine = jnp.asarray(np.sin(np.pi * ((np.arange(NLAT) + 0.5) / NLAT - 0.5)).astype(np.float32))
    return jnp.stack((1.0 / lon, 1.0 / lat, lax.rsqrt((2.0 * lon + 1.0) * (2.0 * lat + 1.0)), sine))


def horner(u, poly):
    total = poly[-1] * u + poly[-2]
    for c in poly[-3::-1]:
        total = total * u + c
    return total


def sine_cosine(turns):
    part = turns - ((turns + MAGIC) - MAGIC)
    h = jnp.abs(part) - 0.25
    u = h * h
    s = horner(u, SIN_POLY)
    return jnp.where(part < 0, -s, s), -h * horner(u, COS_POLY)


def reduce_eight(parts, masks):
    for shift, mask in zip((1, 2, 4), masks):
        merged = []
        for i in range(0, len(parts), 2):
            x, y = parts[i], parts[i + 1]
            merged.append(jnp.where(mask, x, y) + pltpu.roll(jnp.where(mask, y, x), 8 - shift, 0))
        parts = merged
    return parts[0]


def lon_of(place_ref, i):
    return place_ref[HEAD + i]


def lat_of(place_ref, i):
    return place_ref[HEAD + NLAT + i]


def grid_row(place_ref, e):
    return place_ref[0] + e - HLAT


def in_grid(place_ref, e):
    i = grid_row(place_ref, e)
    return jnp.logical_and(i >= 0, i < NLAT)


def safe_row(place_ref, e):
    return jnp.clip(grid_row(place_ref, e), 0, NLAT - 1)


def number_slots(place_ref, slot_row, slot_tap, first_slot, low_tap, high_tap):
    def add_slots(e, lo, hi, count):
        low_tap[e] = lo
        high_tap[e] = hi
        first_slot[e] = count - lo

        def add(a, n):
            slot_row[n] = e
            slot_tap[n] = a
            return n + 1

        return lax.fori_loop(lo, hi + 1, add, count)

    def own_slots(r, count):
        e = r + HLAT
        i = grid_row(place_ref, e)
        h = lat_of(place_ref, i)
        return add_slots(e, jnp.maximum(-h, -i), jnp.minimum(h, NLAT - 1 - i), count)

    own_count = lax.fori_loop(0, ROWS, own_slots, 0)

    def edge_slots(t, count):
        e = jnp.where(t < HLAT, t, t + ROWS)
        h = lat_of(place_ref, safe_row(place_ref, e))
        lo = jnp.maximum(-h, HLAT - e)
        hi = jnp.minimum(h, HLAT + ROWS - 1 - e)
        hi = jnp.where(in_grid(place_ref, e), hi, lo - 1)
        return add_slots(e, lo, hi, count)

    return own_count, lax.fori_loop(0, 2 * HLAT, edge_slots, own_count)


def lay_taps(g, taps, kern, ksum):
    wide = taps.astype(f32)
    at = pl.multiple_of(g * SPAN, 8)
    kern[0, pl.ds(at, SPAN), :] = wide[:, :HALF]
    kern[1, pl.ds(at, SPAN), :] = wide[:, HALF:]
    for q in range(GROUP):
        to = pl.multiple_of((GROUP * g + q) * PAIRS, 8)
        for h in range(2):
            even = kern[h, pl.ds(at + q * TAPS, PAIRS - 4, stride=2), :]
            odd = kern[h, pl.ds(at + q * TAPS + 1, PAIRS - 4, stride=2), :]
            ksum[h, pl.ds(to, PAIRS - 4), :] = even + odd


def network_body(
    place_ref, tab_ref, vec_ref, weight_ref,
    kern, ksum, packed, h1_ref, h2_ref, c2_ref, own_sin_lon, own_cos_lon, own_sin_lat, own_cos_lat,
    slot_row, slot_tap, first_slot, low_tap, high_tap, sin_lon, cos_lon, sin_lat, cos_lat,
):
    own_count, slot_count = number_slots(place_ref, slot_row, slot_tap, first_slot, low_tap, high_tap)
    own_groups = (own_count + GROUP - 1) // GROUP
    tap_index = lax.broadcasted_iota(jnp.int32, (TAPS, C), 0)
    lat_index = (lax.broadcasted_iota(jnp.int32, (16, C), 0) - HLAT).astype(f32)
    fw = vec_ref[0:3]
    first_bias = vec_ref[3:4]
    hidden_bias = vec_ref[4:5] * TURN
    output_bias = vec_ref[5:6]
    omega = 30.0 * TURN

    def angles(e, _):
        @pl.when(in_grid(place_ref, e))
        def _():
            i = safe_row(place_ref, e)
            w = lon_of(place_ref, i)
            lon = (tap_index - w).astype(f32) * tab_ref[0, i]
            phase = (lon * fw[0:1] + (tab_ref[3, i] * fw[2:3] + first_bias)) * omega
            s, c = sine_cosine(phase)
            sin_lon[e] = s
            cos_lon[e] = c
            s, c = sine_cosine((lat_index * tab_ref[1, i]) * fw[1:2] * omega)
            sin_lat[e] = s
            cos_lat[e] = c

        return 0

    lax.fori_loop(0, EXT, angles, 0)

    def network(g, _):
        pos = [jnp.minimum(GROUP * g + q, slot_count - 1) for q in range(GROUP)]
        rows = [slot_row[n] for n in pos]
        hidden = []
        for n, e in zip(pos, rows):
            t = slot_tap[n] + HLAT
            hidden.append(sin_lon[e] * cos_lat[e, pl.ds(t, 1), :] + cos_lon[e] * sin_lat[e, pl.ds(t, 1), :])
        h1 = jnp.concatenate(hidden, axis=0).astype(bf16)
        pre = jnp.dot(h1, weight_ref[0], preferred_element_type=f32) * TURN + hidden_bias
        s, c = sine_cosine(pre)
        h2 = s.astype(bf16)

        @pl.when(g < own_groups)
        def _():
            h1_ref[g] = h1
            h2_ref[g] = h2
            c2_ref[g] = c

        raw = jnp.dot(h2, weight_ref[1], preferred_element_type=f32) + output_bias
        taps = []
        for q in range(GROUP):
            i = safe_row(place_ref, rows[q])
            limit = 2 * lon_of(place_ref, i)
            taps.append(jnp.where(tap_index <= limit, raw[q * TAPS:(q + 1) * TAPS] * tab_ref[2, i], 0.0))
        taps = jnp.concatenate(taps, axis=0).astype(bf16)
        packed[g] = taps
        lay_taps(g, taps, kern, ksum)
        return 0

    lax.fori_loop(0, (slot_count + GROUP - 1) // GROUP, network, 0)
    for own, every in (
        (own_sin_lon, sin_lon), (own_cos_lon, cos_lon), (own_sin_lat, sin_lat), (own_cos_lat, cos_lat),
    ):
        own[...] = every[HLAT:HLAT + ROWS]


def network_pass(place, table, vectors, weights):
    smem = pl.BlockSpec(memory_space=pltpu.SMEM)
    vmem = pl.BlockSpec(memory_space=pltpu.VMEM)
    return pl.pallas_call(
        network_body,
        out_shape=(
            jax.ShapeDtypeStruct((2, SLOTS * TAPS, HALF), f32),
            jax.ShapeDtypeStruct((2, SLOTS * PAIRS, HALF), f32),
            jax.ShapeDtypeStruct((SLOTS // GROUP, SPAN, C), bf16),
            jax.ShapeDtypeStruct((OWN // GROUP, SPAN, C), bf16),
            jax.ShapeDtypeStruct((OWN // GROUP, SPAN, C), bf16),
            jax.ShapeDtypeStruct((OWN // GROUP, SPAN, C), f32),
            jax.ShapeDtypeStruct((ROWS, TAPS, C), f32),
            jax.ShapeDtypeStruct((ROWS, TAPS, C), f32),
            jax.ShapeDtypeStruct((ROWS, 16, C), f32),
            jax.ShapeDtypeStruct((ROWS, 16, C), f32),
        ),
        in_specs=[smem] * 2 + [vmem] * 2,
        out_specs=(vmem,) * 10,
        scratch_shapes=[
            pltpu.SMEM((SLOTS + 8,), jnp.int32),
            pltpu.SMEM((SLOTS + 8,), jnp.int32),
            pltpu.SMEM((16,), jnp.int32),
            pltpu.SMEM((16,), jnp.int32),
            pltpu.SMEM((16,), jnp.int32),
            pltpu.VMEM((EXT, TAPS, C), f32),
            pltpu.VMEM((EXT, TAPS, C), f32),
            pltpu.VMEM((EXT, 16, C), f32),
            pltpu.VMEM((EXT, 16, C), f32),
        ],
        compiler_params=pltpu.CompilerParams(vmem_limit_bytes=16 * 1024 * 1024),
        cost_estimate=pl.CostEstimate(flops=6_000_000_000, bytes_accessed=16_000_000, transcendentals=0),
        name="network_pass",
    )(place, table, vectors, weights)


def build_windows(place_ref, here_ref, inner_ref, outer_ref, which, front, line, window, change):
    lat_odd = place_ref[2] == 1
    left_inner = place_ref[1] == 1

    def one(e, _):
        @pl.when(in_grid(place_ref, e))
        def _():
            band = e // ROWS
            part = jnp.where(band == 1, 0, jnp.where((band == 2) == lat_odd, 2, 1))
            row = e % ROWS
            for n in range(2):
                lanes = slice(n * HALF, (n + 1) * HALF)
                near = inner_ref[part, which, row, :, lanes].astype(f32)
                far = outer_ref[part, which, row, :, lanes].astype(f32)
                line[n, 0:8] = jnp.zeros((8, HALF), f32)
                line[n, 96:LINE] = jnp.zeros((LINE - 96, HALF), f32)
                line[n, front:front + 32] = jnp.where(left_inner, near, far)
                line[n, front + 32:front + 64] = here_ref[part, which, row, :, lanes].astype(f32)
                line[n, front + 64:front + 96] = jnp.where(left_inner, far, near)
            for n in range(2):
                last = None
                for p in range(WIN):
                    value = line[n, pl.ds(p, 8, stride=4), :]
                    window[e, n, p] = value
                    if p:
                        change[e, n, p - 1] = last - value
                    last = value

        return 0

    lax.fori_loop(0, EXT, one, 0)


def taps_of(window, change, e, n, start):
    odd = [window[e, n, start + 2 * i + 1] for i in range(5)]
    fall = [change[e, n, start + 2 * i] for i in range(5)]
    next_fall = [change[e, n, start + 2 * i + 1] for i in range(5)]
    return odd, fall, next_fall


def row_of(source, h, at):
    return source[h, pl.ds(at, 8, stride=0), :]


def combine(total):
    p0, p1, q0, q1, r0, r1 = total
    return p0 + q0, p0 - r0, p1 + q1, p1 - r1


def gradient_body(
    place_ref, tab_ref, here_ref, inner_ref, outer_ref, cot_ref, weight_ref,
    kern, ksum, h1_ref, h2_ref, c2_ref, sin_lon, cos_lon, sin_lat, cos_lat,
    keep_ref, send_ref,
    slot_row, slot_tap, first_slot, low_tap, high_tap,
    line, window, change, mine_line, grad, conv, d_mix, d_out, d_hid, d_small, d_side,
):
    inverse = 1.0 / math.sqrt(NLAT * NLON)
    own_count, slot_count = number_slots(place_ref, slot_row, slot_tap, first_slot, low_tap, high_tap)
    tap_index = lax.broadcasted_iota(jnp.int32, (TAPS, C), 0)
    core = place_ref[1]
    for h in range(2):
        mine_line[h] = here_ref[0, 1, :, :, h * HALF:(h + 1) * HALF].reshape(ROWS * COLS, HALF).astype(f32)
    build_windows(place_ref, here_ref, inner_ref, outer_ref, 0, 0, line, window, change)
    sub = lax.broadcasted_iota(jnp.int32, (8, HALF), 0)
    masks = [(sub & bit) == 0 for bit in (1, 2, 4)]
    zero = jnp.zeros((8, HALF), f32)

    def conv_row(r, _):
        e = r + HLAT
        w = lon_of(place_ref, grid_row(place_ref, e))
        blocks = (2 * w + 8) // 8
        mine = [[mine_line[h, pl.ds(r * COLS + t, 8, stride=4), :] for t in range(4)] for h in range(2)]
        both = [[m[0] + m[1], m[2] + m[3]] for m in mine]

        def one_lat(a, total):
            slot = first_slot[e] + a

            def one_block(b, total):
                new = []
                start = HLON - w + 8 * b
                at = slot * TAPS + 8 * b
                pair = slot * PAIRS + 4 * b
                for h in range(2):
                    acc = list(total[6 * h:6 * h + 6])
                    odd, fall, next_fall = taps_of(window, change, e + a, h, start)
                    parts = []
                    for j in range(4):
                        k_sum = row_of(ksum, h, pair + j)
                        k_even = row_of(kern, h, at + 2 * j)
                        k_odd = row_of(kern, h, at + 2 * j + 1)
                        for m in range(2):
                            acc[m] = acc[m] + k_sum * odd[m + j]
                            acc[2 + m] = acc[2 + m] + k_even * fall[m + j]
                            acc[4 + m] = acc[4 + m] + k_odd * next_fall[m + j]
                        p = both[h][0] * odd[j] + both[h][1] * odd[j + 1]
                        parts.append(p + (mine[h][0] * fall[j] + mine[h][2] * fall[j + 1]))
                        parts.append(p - (mine[h][1] * next_fall[j] + mine[h][3] * next_fall[j + 1]))
                    grad[h, pl.ds(pl.multiple_of(at, 8), 8), :] = reduce_eight(parts, masks)
                    new += acc
                return tuple(new)

            return lax.fori_loop(0, blocks, one_block, total)

        total = lax.fori_loop(low_tap[e], high_tap[e] + 1, one_lat, (zero,) * 12)
        for h in range(2):
            for t, value in enumerate(combine(total[6 * h:6 * h + 6])):
                conv[h, pl.ds(r * COLS + t, 8, stride=4), :] = value
        return 0

    lax.fori_loop(0, ROWS, conv_row, 0)
    for h in range(2):
        d_mix[h * HALF:(h + 1) * HALF, :] = lax.dot_general(
            conv[h].astype(bf16), cot_ref[...], (((0,), (0,)), ((), ())), preferred_element_type=f32
        )

    d_out[...] = jnp.zeros_like(d_out)
    d_hid[...] = jnp.zeros_like(d_hid)
    d_small[...] = jnp.zeros_like(d_small)

    def adjoint(g, _):
        raw = []
        pos = [jnp.minimum(GROUP * g + q, own_count - 1) for q in range(GROUP)]
        rows = [slot_row[n] for n in pos]
        for q in range(GROUP):
            i = grid_row(place_ref, rows[q])
            w = lon_of(place_ref, i)
            norm = tab_ref[2, i]
            limit = jnp.where(GROUP * g + q < own_count, 2 * w, -1)
            at = pl.multiple_of(pos[q] * TAPS, 8)
            part = jnp.concatenate([grad[0, pl.ds(at, TAPS), :], grad[1, pl.ds(at, TAPS), :]], axis=1)
            raw.append(jnp.where(tap_index <= limit, part * norm, 0.0))
        raw = jnp.concatenate(raw, axis=0)
        raw_low = raw.astype(bf16)
        h1 = h1_ref[g]
        h2 = h2_ref[g]
        rows_by_rows = (((0,), (0,)), ((), ()))
        d_out[...] += lax.dot_general(h2, raw_low, rows_by_rows, preferred_element_type=f32)
        d_small[5:6, :] += jnp.sum(raw, axis=0, keepdims=True)
        gp = lax.dot_general(
            raw_low, weight_ref[1], (((1,), (1,)), ((), ())), preferred_element_type=f32
        ) * c2_ref[g]
        gp_low = gp.astype(bf16)
        d_hid[...] += lax.dot_general(h1, gp_low, rows_by_rows, preferred_element_type=f32)
        d_small[4:5, :] += jnp.sum(gp, axis=0, keepdims=True)
        gf = lax.dot_general(
            gp_low, weight_ref[0], (((1,), (1,)), ((), ())), preferred_element_type=f32
        )
        for q in range(GROUP):
            e = rows[q]
            i = grid_row(place_ref, e)
            w = lon_of(place_ref, i)
            a = slot_tap[pos[q]]
            t = a + HLAT
            c1 = cos_lon[e - HLAT] * cos_lat[e - HLAT, pl.ds(t, 1), :] - sin_lon[e - HLAT] * sin_lat[e - HLAT, pl.ds(t, 1), :]
            gq = gf[q * TAPS:(q + 1) * TAPS] * c1
            lon = (tap_index - w).astype(f32) * tab_ref[0, i]
            total = jnp.sum(gq, axis=0, keepdims=True)
            d_small[0:1, :] += jnp.sum(gq * lon, axis=0, keepdims=True)
            d_small[1:2, :] += total * (a.astype(f32) * tab_ref[1, i])
            d_small[2:3, :] += total * tab_ref[3, i]
            d_small[3:4, :] += total
        return 0

    lax.fori_loop(0, (own_count + GROUP - 1) // GROUP, adjoint, 0)
    d_small[0:4, :] = d_small[0:4, :] * 30.0
    d_side[...] = jnp.transpose(d_small[...])
    for target, half in ((keep_ref, core), (send_ref, 1 - core)):
        rows = pl.ds(pl.multiple_of(half * HALF, HALF), HALF)
        for q, source in enumerate((d_mix, d_hid, d_out, d_side)):
            part = source[rows, :] * inverse
            target[:, q * C:q * C + part.shape[1]] = part.astype(bf16)


def back_body(
    place_ref, here_ref, inner_ref, outer_ref, packed, gfield_ref,
    slot_row, slot_tap, first_slot, low_tap, high_tap, line, window, change, kern, ksum, back,
):
    _, slot_count = number_slots(place_ref, slot_row, slot_tap, first_slot, low_tap, high_tap)

    def lay(g, _):
        lay_taps(g, packed[g], kern, ksum)
        return 0

    lax.fori_loop(0, (slot_count + GROUP - 1) // GROUP, lay, 0)
    build_windows(place_ref, here_ref, inner_ref, outer_ref, 1, 8, line, window, change)
    zero = jnp.zeros((8, HALF), f32)

    def back_row(r, _):
        def one_source(e, total):
            a = r + HLAT - e
            i = safe_row(place_ref, e)
            w = lon_of(place_ref, i)
            live = jnp.logical_and(in_grid(place_ref, e), jnp.abs(a) <= lat_of(place_ref, i))
            blocks = jnp.where(live, (2 * w + 8) // 8, 0)
            slot = first_slot[e] + a

            def one_block(b, total):
                start = HLON + 1 + w - 8 * b
                at = slot * TAPS + 8 * b
                pair = slot * PAIRS + 4 * b
                new = []
                for h in range(2):
                    acc = list(total[6 * h:6 * h + 6])
                    odd, fall, next_fall = taps_of(window, change, e, h, start)
                    for j in range(4):
                        k_sum = row_of(ksum, h, pair + 3 - j)
                        k_even = row_of(kern, h, at + 7 - 2 * j)
                        k_odd = row_of(kern, h, at + 6 - 2 * j)
                        for m in range(2):
                            acc[m] = acc[m] + k_sum * odd[m + j]
                            acc[2 + m] = acc[2 + m] + k_even * fall[m + j]
                            acc[4 + m] = acc[4 + m] + k_odd * next_fall[m + j]
                    new += acc
                return tuple(new)

            return lax.fori_loop(0, blocks, one_block, total)

        total = lax.fori_loop(r, r + TLAT, one_source, (zero,) * 12)
        for h in range(2):
            for t, value in enumerate(combine(total[6 * h:6 * h + 6])):
                back[h, pl.ds(r * COLS + t, 8, stride=4), :] = value
        return 0

    lax.fori_loop(0, ROWS, back_row, 0)
    for h in range(2):
        gfield_ref[:, h * HALF:(h + 1) * HALF] = back[h].astype(bf16)


def unpack_body(place_ref, own_ref, other_ref, mix_ref, hid_ref, out_ref, first_ref, fb_ref, hb_ref, ob_ref, side):
    core = place_ref[1]
    for source, half in ((own_ref, core), (other_ref, 1 - core)):
        rows = pl.ds(pl.multiple_of(half * HALF, HALF), HALF)
        for q, target in enumerate((mix_ref, hid_ref, out_ref)):
            target[rows, :] = source[:, q * C:(q + 1) * C].astype(f32)
        side[rows, :] = source[:, 3 * C:].astype(f32)
    small = jnp.transpose(side[...])
    first_ref[...] = small[0:3]
    fb_ref[...] = small[3:4]
    hb_ref[...] = small[4:5]
    ob_ref[...] = small[5:6]


def unpack(place, own, other):
    vmem = pl.BlockSpec(memory_space=pltpu.VMEM)
    square = jax.ShapeDtypeStruct((C, C), f32)
    line = jax.ShapeDtypeStruct((1, C), f32)
    return pl.pallas_call(
        unpack_body,
        out_shape=(square, square, square, jax.ShapeDtypeStruct((3, C), f32), line, line, line),
        in_specs=[pl.BlockSpec(memory_space=pltpu.SMEM)] + [vmem] * 2,
        out_specs=(vmem,) * 7,
        scratch_shapes=[pltpu.VMEM((C, HALF), f32)],
        compiler_params=pltpu.CompilerParams(vmem_limit_bytes=8 * 1024 * 1024),
        name="unpack",
    )(place, own, other)


def slot_scratch():
    return [
        pltpu.SMEM((SLOTS + 8,), jnp.int32),
        pltpu.SMEM((SLOTS + 8,), jnp.int32),
        pltpu.SMEM((16,), jnp.int32),
        pltpu.SMEM((16,), jnp.int32),
        pltpu.SMEM((16,), jnp.int32),
    ]


def gradient_pass(place, table, here, inner, outer, cotangent, weights, saved):
    smem = pl.BlockSpec(memory_space=pltpu.SMEM)
    vmem = pl.BlockSpec(memory_space=pltpu.VMEM)
    return pl.pallas_call(
        gradient_body,
        out_shape=(
            jax.ShapeDtypeStruct((C // 2, PACK), bf16),
            jax.ShapeDtypeStruct((C // 2, PACK), bf16),
        ),
        in_specs=[smem] * 2 + [vmem] * 14,
        out_specs=(vmem,) * 2,
        scratch_shapes=slot_scratch() + [
            pltpu.VMEM((2, LINE, HALF), f32),
            pltpu.VMEM((EXT, 2, WIN, 8, HALF), f32),
            pltpu.VMEM((EXT, 2, WIN, 8, HALF), f32),
            pltpu.VMEM((2, ROWS * COLS, HALF), f32),
            pltpu.VMEM((2, OWN * TAPS, HALF), f32),
            pltpu.VMEM((2, ROWS * COLS, HALF), f32),
            pltpu.VMEM((C, C), f32),
            pltpu.VMEM((C, C), f32),
            pltpu.VMEM((C, C), f32),
            pltpu.VMEM((HALF, C), f32),
            pltpu.VMEM((C, HALF), f32),
        ],
        compiler_params=pltpu.CompilerParams(vmem_limit_bytes=26 * 1024 * 1024),
        cost_estimate=pl.CostEstimate(flops=9_000_000_000, bytes_accessed=20_000_000, transcendentals=0),
        name="gradient_pass",
    )(place, table, here, inner, outer, cotangent, weights, *saved)


def back_pass(place, here, inner, outer, packed):
    smem = pl.BlockSpec(memory_space=pltpu.SMEM)
    vmem = pl.BlockSpec(memory_space=pltpu.VMEM)
    return pl.pallas_call(
        back_body,
        out_shape=jax.ShapeDtypeStruct((ROWS * COLS, C), bf16),
        in_specs=[smem] + [vmem] * 4,
        out_specs=vmem,
        scratch_shapes=slot_scratch() + [
            pltpu.VMEM((2, LINE, HALF), f32),
            pltpu.VMEM((EXT, 2, WIN, 8, HALF), f32),
            pltpu.VMEM((EXT, 2, WIN, 8, HALF), f32),
            pltpu.VMEM((2, SLOTS * TAPS, HALF), f32),
            pltpu.VMEM((2, SLOTS * PAIRS, HALF), f32),
            pltpu.VMEM((2, ROWS * COLS, HALF), f32),
        ],
        compiler_params=pltpu.CompilerParams(vmem_limit_bytes=28 * 1024 * 1024),
        cost_estimate=pl.CostEstimate(flops=4_000_000_000, bytes_accessed=8_000_000, transcendentals=0),
        name="back_pass",
    )(place, here, inner, outer, packed)


def core_add_body(keep_ref, other_ref, total_ref):
    total_ref[...] = (keep_ref[...].astype(f32) + other_ref[...].astype(f32)).astype(bf16)


def core_add(keep, other):
    vmem = pl.BlockSpec(memory_space=pltpu.VMEM)
    return pl.pallas_call(
        core_add_body,
        out_shape=jax.ShapeDtypeStruct(keep.shape, bf16),
        in_specs=[vmem] * 2,
        out_specs=vmem,
        compiler_params=pltpu.CompilerParams(vmem_limit_bytes=4 * 1024 * 1024),
        name="core_add",
    )(keep, other)


def swap(block, axis, pairs):
    return lax.ppermute(block, axis, pairs)


LAT_INNER = [(i, i ^ 1) for i in range(8)]
LAT_OUTER = [(i, i + 1 if i % 2 else i - 1) for i in range(1, 7)]
LON_INNER = [(i, i ^ 1) for i in range(32)]
LON_OUTER = [(i, (i + 1 if i % 2 else i - 1) % 32) for i in range(32)]
PLANE = ("y", "x_low", "x_high")


def spread(block, axis):
    return lax.all_to_all(block, axis, 0, 0, tiled=True)


LAT = ("y", "x_low")
LON = ("z", "x_high", "core")
CORE = [(0, 1), (1, 0)]


def beside(block):
    return jnp.stack((block, swap(block, LAT, LAT_INNER), swap(block, LAT, LAT_OUTER)), axis=0)


def around(here):
    return here, swap(here, LON, LON_INNER), swap(here, LON, LON_OUTER)


def z_add(total, bits):
    return total + swap(total, "z", [(i, i ^ bits) for i in range(8)])


def shards(
    field, cotangent, mix_weight, first_weight, first_bias, hidden_weight, hidden_bias,
    output_weight, output_bias, lon_half, lat_half,
):
    flat_cot = cotangent.reshape(-1, C)
    mixed = lax.dot_general(
        flat_cot, mix_weight, (((1,), (1,)), ((), ())), preferred_element_type=f32
    ).astype(bf16)
    parts = around(beside(jnp.stack((field, mixed.reshape(ROWS, COLS, C)), axis=0)))
    lat = lax.axis_index("y") * 2 + lax.axis_index("x_low")
    place = jnp.stack((lat * ROWS, lax.axis_index("core"), lat % 2)).astype(jnp.int32)
    place = jnp.concatenate((place, lon_half, lat_half))
    table = tables(lon_half, lat_half)
    vectors = jnp.concatenate((first_weight, jnp.stack((first_bias, hidden_bias, output_bias))), axis=0)
    weights = jnp.stack((hidden_weight, output_weight))
    kern, ksum, packed, *saved = network_pass(place, table, vectors, weights)
    keep, send = gradient_pass(place, table, *parts, flat_cot, weights, (kern, ksum, *saved))
    total = core_add(keep, swap(send, "core", CORE))
    total, parts = lax.optimization_barrier((total, parts))
    total = spread(total.reshape(16, 8, PACK), PLANE)
    back = back_pass(place, *parts, packed)
    total, back = lax.optimization_barrier((total, back))
    total = jnp.sum(total.astype(f32), axis=0)
    for bits in (1, 2, 6):
        total = z_add(total, bits)
    own = spread(jnp.broadcast_to(total.astype(bf16)[None], (16, 8, PACK)), PLANE).reshape(HALF, PACK)
    mix, hid, out, first, fb, hb, ob = unpack(place, own, swap(own, "core", CORE))
    return (
        back.reshape(ROWS, COLS, C), mix, first, fb.reshape(C), hid, hb.reshape(C), out, ob.reshape(C),
    )


def solution(mesh):
    split = Mesh(mesh.devices.reshape(8, 2, 2, 4, 2), ("z", "x_high", "core", "y", "x_low"))
    grid = P(LAT, LON, None)
    in_specs = (grid, grid) + (P(),) * 9
    out_specs = (grid,) + (P(),) * 7
    return jax.shard_map(shards, mesh=split, in_specs=in_specs, out_specs=out_specs, check_vma=False)
```

```python
import functools
import math

import jax
import jax.numpy as jnp
import numpy as np
from jax import lax
from jax.experimental import pallas as pl
from jax.experimental.pallas import tpu as pltpu
from jax.sharding import Mesh
from jax.sharding import PartitionSpec as P

HLON = 32
HLAT = 4
NLAT = 32
NLON = 1024
ROWS = 4
COLS = 32
EXT = ROWS + 2 * HLAT
C = 256
HALF = 128
TAPS = 72
TLAT = 2 * HLAT + 1
GROUP = 4
SPAN = GROUP * TAPS
SLOTS = 56
OWN = ROWS * TLAT
WIN = 76
PAIRS = 40
HEAD = 3
LINE = 104
PACK = 3 * C + HALF
MAGIC = 12582912.0
TURN = 1.0 / (2.0 * math.pi)

f32 = jnp.float32
bf16 = jnp.bfloat16

SIN_POLY = (0.99999995, -19.73917132, 64.93458165, -85.24010036, 56.24054044)
COS_POLY = (6.28318528, -41.34168067, 81.60248074, -76.58128456, 39.76072208)


def tables(lon_half, lat_half):
    lon, lat = lon_half.astype(f32), lat_half.astype(f32)
    sine = jnp.asarray(np.sin(np.pi * ((np.arange(NLAT) + 0.5) / NLAT - 0.5)).astype(np.float32))
    return jnp.stack((1.0 / lon, 1.0 / lat, lax.rsqrt((2.0 * lon + 1.0) * (2.0 * lat + 1.0)), sine))


def horner(u, poly):
    total = poly[-1] * u + poly[-2]
    for c in poly[-3::-1]:
        total = total * u + c
    return total


def sine_cosine(turns):
    part = turns - ((turns + MAGIC) - MAGIC)
    h = jnp.abs(part) - 0.25
    u = h * h
    s = horner(u, SIN_POLY)
    return jnp.where(part < 0, -s, s), -h * horner(u, COS_POLY)


def reduce_eight(parts, masks):
    for shift, mask in zip((1, 2, 4), masks):
        merged = []
        for i in range(0, len(parts), 2):
            x, y = parts[i], parts[i + 1]
            merged.append(jnp.where(mask, x, y) + pltpu.roll(jnp.where(mask, y, x), 8 - shift, 0))
        parts = merged
    return parts[0]


def lon_of(place_ref, i):
    return place_ref[HEAD + i]


def lat_of(place_ref, i):
    return place_ref[HEAD + NLAT + i]


def grid_row(place_ref, e):
    return place_ref[0] + e - HLAT


def in_grid(place_ref, e):
    i = grid_row(place_ref, e)
    return jnp.logical_and(i >= 0, i < NLAT)


def safe_row(place_ref, e):
    return jnp.clip(grid_row(place_ref, e), 0, NLAT - 1)


def number_slots(place_ref, slot_row, slot_tap, first_slot, low_tap, high_tap):
    def add_slots(e, lo, hi, count):
        low_tap[e] = lo
        high_tap[e] = hi
        first_slot[e] = count - lo

        def add(a, n):
            slot_row[n] = e
            slot_tap[n] = a
            return n + 1

        return lax.fori_loop(lo, hi + 1, add, count)

    def own_slots(r, count):
        e = r + HLAT
        i = grid_row(place_ref, e)
        h = lat_of(place_ref, i)
        return add_slots(e, jnp.maximum(-h, -i), jnp.minimum(h, NLAT - 1 - i), count)

    own_count = lax.fori_loop(0, ROWS, own_slots, 0)

    def edge_slots(t, count):
        e = jnp.where(t < HLAT, t, t + ROWS)
        h = lat_of(place_ref, safe_row(place_ref, e))
        lo = jnp.maximum(-h, HLAT - e)
        hi = jnp.minimum(h, HLAT + ROWS - 1 - e)
        hi = jnp.where(in_grid(place_ref, e), hi, lo - 1)
        return add_slots(e, lo, hi, count)

    return own_count, lax.fori_loop(0, 2 * HLAT, edge_slots, own_count)


def lay_taps(g, taps, kern, ksum):
    wide = taps.astype(f32)
    at = pl.multiple_of(g * SPAN, 8)
    for h in range(kern.shape[0]):
        kern[h, pl.ds(at, SPAN), :] = wide[:, h * HALF:(h + 1) * HALF]
    for q in range(GROUP):
        to = pl.multiple_of((GROUP * g + q) * PAIRS, 8)
        for h in range(kern.shape[0]):
            even = kern[h, pl.ds(at + q * TAPS, PAIRS - 4, stride=2), :]
            odd = kern[h, pl.ds(at + q * TAPS + 1, PAIRS - 4, stride=2), :]
            ksum[h, pl.ds(to, PAIRS - 4), :] = even + odd


def network_body(
    place_ref, tab_ref, vec_ref, weight_ref,
    kern, ksum, packed, h1_ref, h2_ref, c2_ref, own_sin_lon, own_cos_lon, own_sin_lat, own_cos_lat,
    slot_row, slot_tap, first_slot, low_tap, high_tap, sin_lon, cos_lon, sin_lat, cos_lat,
):
    own_count, slot_count = number_slots(place_ref, slot_row, slot_tap, first_slot, low_tap, high_tap)
    own_groups = (own_count + GROUP - 1) // GROUP
    tap_index = lax.broadcasted_iota(jnp.int32, (TAPS, C), 0)
    lat_index = (lax.broadcasted_iota(jnp.int32, (16, C), 0) - HLAT).astype(f32)
    fw = vec_ref[0:3]
    first_bias = vec_ref[3:4]
    hidden_bias = vec_ref[4:5] * TURN
    output_bias = vec_ref[5:6]
    omega = 30.0 * TURN

    def angles(e, _):
        @pl.when(in_grid(place_ref, e))
        def _():
            i = safe_row(place_ref, e)
            w = lon_of(place_ref, i)
            lon = (tap_index - w).astype(f32) * tab_ref[0, i]
            phase = (lon * fw[0:1] + (tab_ref[3, i] * fw[2:3] + first_bias)) * omega
            s, c = sine_cosine(phase)
            sin_lon[e] = s
            cos_lon[e] = c
            s, c = sine_cosine((lat_index * tab_ref[1, i]) * fw[1:2] * omega)
            sin_lat[e] = s
            cos_lat[e] = c

        return 0

    lax.fori_loop(0, EXT, angles, 0)

    def network(g, _):
        pos = [jnp.minimum(GROUP * g + q, slot_count - 1) for q in range(GROUP)]
        rows = [slot_row[n] for n in pos]
        hidden = []
        for n, e in zip(pos, rows):
            t = slot_tap[n] + HLAT
            hidden.append(sin_lon[e] * cos_lat[e, pl.ds(t, 1), :] + cos_lon[e] * sin_lat[e, pl.ds(t, 1), :])
        h1 = jnp.concatenate(hidden, axis=0).astype(bf16)
        pre = jnp.dot(h1, weight_ref[0], preferred_element_type=f32) * TURN + hidden_bias
        s, c = sine_cosine(pre)
        h2 = s.astype(bf16)

        @pl.when(g < own_groups)
        def _():
            h1_ref[g] = h1
            h2_ref[g] = h2
            c2_ref[g] = c

        raw = jnp.dot(h2, weight_ref[1], preferred_element_type=f32) + output_bias
        taps = []
        for q in range(GROUP):
            i = safe_row(place_ref, rows[q])
            limit = 2 * lon_of(place_ref, i)
            taps.append(jnp.where(tap_index <= limit, raw[q * TAPS:(q + 1) * TAPS] * tab_ref[2, i], 0.0))
        taps = jnp.concatenate(taps, axis=0).astype(bf16)
        packed[g] = taps
        lay_taps(g, taps, kern, ksum)
        return 0

    lax.fori_loop(0, (slot_count + GROUP - 1) // GROUP, network, 0)
    for own, every in (
        (own_sin_lon, sin_lon), (own_cos_lon, cos_lon), (own_sin_lat, sin_lat), (own_cos_lat, cos_lat),
    ):
        own[...] = every[HLAT:HLAT + ROWS]


def network_pass(place, table, vectors, weights):
    smem = pl.BlockSpec(memory_space=pltpu.SMEM)
    vmem = pl.BlockSpec(memory_space=pltpu.VMEM)
    return pl.pallas_call(
        network_body,
        out_shape=(
            jax.ShapeDtypeStruct((2, SLOTS * TAPS, HALF), f32),
            jax.ShapeDtypeStruct((2, SLOTS * PAIRS, HALF), f32),
            jax.ShapeDtypeStruct((SLOTS // GROUP, SPAN, C), bf16),
            jax.ShapeDtypeStruct((OWN // GROUP, SPAN, C), bf16),
            jax.ShapeDtypeStruct((OWN // GROUP, SPAN, C), bf16),
            jax.ShapeDtypeStruct((OWN // GROUP, SPAN, C), f32),
            jax.ShapeDtypeStruct((ROWS, TAPS, C), f32),
            jax.ShapeDtypeStruct((ROWS, TAPS, C), f32),
            jax.ShapeDtypeStruct((ROWS, 16, C), f32),
            jax.ShapeDtypeStruct((ROWS, 16, C), f32),
        ),
        in_specs=[smem] * 2 + [vmem] * 2,
        out_specs=(vmem,) * 10,
        scratch_shapes=[
            pltpu.SMEM((SLOTS + 8,), jnp.int32),
            pltpu.SMEM((SLOTS + 8,), jnp.int32),
            pltpu.SMEM((16,), jnp.int32),
            pltpu.SMEM((16,), jnp.int32),
            pltpu.SMEM((16,), jnp.int32),
            pltpu.VMEM((EXT, TAPS, C), f32),
            pltpu.VMEM((EXT, TAPS, C), f32),
            pltpu.VMEM((EXT, 16, C), f32),
            pltpu.VMEM((EXT, 16, C), f32),
        ],
        compiler_params=pltpu.CompilerParams(vmem_limit_bytes=16 * 1024 * 1024),
        cost_estimate=pl.CostEstimate(flops=6_000_000_000, bytes_accessed=16_000_000, transcendentals=0),
        name="network_pass",
    )(place, table, vectors, weights)


def build_windows(place_ref, read_here, read_inner, read_outer, halves, front, line, window, change):
    lat_odd = place_ref[2] == 1
    left_inner = place_ref[1] == 1

    def one(e, _):
        @pl.when(in_grid(place_ref, e))
        def _():
            band = e // ROWS
            part = jnp.where(band == 1, 0, jnp.where((band == 2) == lat_odd, 2, 1))
            row = e % ROWS
            for n, h in enumerate(halves):
                lanes = slice(h * HALF, (h + 1) * HALF)
                near = read_inner(part, row, lanes).astype(f32)
                far = read_outer(part, row, lanes).astype(f32)
                line[n, 0:8] = jnp.zeros((8, HALF), f32)
                line[n, 96:LINE] = jnp.zeros((LINE - 96, HALF), f32)
                line[n, front:front + 32] = jnp.where(left_inner, near, far)
                line[n, front + 32:front + 64] = read_here(part, row, lanes).astype(f32)
                line[n, front + 64:front + 96] = jnp.where(left_inner, far, near)
            for n in range(len(halves)):
                last = None
                for p in range(WIN):
                    value = line[n, pl.ds(p, 8, stride=4), :]
                    window[e, n, p] = value
                    if p:
                        change[e, n, p - 1] = last - value
                    last = value

        return 0

    lax.fori_loop(0, EXT, one, 0)


def taps_of(window, change, e, n, start):
    odd = [window[e, n, start + 2 * i + 1] for i in range(5)]
    fall = [change[e, n, start + 2 * i] for i in range(5)]
    next_fall = [change[e, n, start + 2 * i + 1] for i in range(5)]
    return odd, fall, next_fall


def row_of(source, h, at):
    return source[h, pl.ds(at, 8, stride=0), :]


def combine(total):
    p0, p1, q0, q1, r0, r1 = total
    return p0 + q0, p0 - r0, p1 + q1, p1 - r1


def gradient_body(
    place_ref, tab_ref, here_ref, inner_ref, outer_ref, cot_ref, weight_ref,
    kern, ksum, h1_ref, h2_ref, c2_ref, sin_lon, cos_lon, sin_lat, cos_lat,
    keep_ref, send_ref, cots_ref,
    slot_row, slot_tap, first_slot, low_tap, high_tap,
    line, window, change, mine_line, grad, conv, d_mix, d_out, d_hid, d_small, d_side,
):
    inverse = 1.0 / math.sqrt(NLAT * NLON)
    own_count, slot_count = number_slots(place_ref, slot_row, slot_tap, first_slot, low_tap, high_tap)
    tap_index = lax.broadcasted_iota(jnp.int32, (TAPS, C), 0)
    core = place_ref[1]
    for h in range(2):
        mine_line[h] = here_ref[0, 1, :, :, h * HALF:(h + 1) * HALF].reshape(ROWS * COLS, HALF).astype(f32)
    def reader(ref):
        return lambda part, row, lanes: ref[part, 0, row, :, lanes]

    for n, ref in enumerate((here_ref, inner_ref, outer_ref)):
        cots_ref[n] = ref[:, 1]
    build_windows(
        place_ref, reader(here_ref), reader(inner_ref), reader(outer_ref), (0, 1), 0, line, window, change
    )
    sub = lax.broadcasted_iota(jnp.int32, (8, HALF), 0)
    masks = [(sub & bit) == 0 for bit in (1, 2, 4)]
    zero = jnp.zeros((8, HALF), f32)

    def conv_row(r, _):
        e = r + HLAT
        w = lon_of(place_ref, grid_row(place_ref, e))
        blocks = (2 * w + 8) // 8
        mine = [[mine_line[h, pl.ds(r * COLS + t, 8, stride=4), :] for t in range(4)] for h in range(2)]
        both = [[m[0] + m[1], m[2] + m[3]] for m in mine]

        def one_lat(a, total):
            slot = first_slot[e] + a

            def one_block(b, total):
                new = []
                start = HLON - w + 8 * b
                at = slot * TAPS + 8 * b
                pair = slot * PAIRS + 4 * b
                for h in range(2):
                    acc = list(total[6 * h:6 * h + 6])
                    odd, fall, next_fall = taps_of(window, change, e + a, h, start)
                    parts = []
                    for j in range(4):
                        k_sum = row_of(ksum, h, pair + j)
                        k_even = row_of(kern, h, at + 2 * j)
                        k_odd = row_of(kern, h, at + 2 * j + 1)
                        for m in range(2):
                            acc[m] = acc[m] + k_sum * odd[m + j]
                            acc[2 + m] = acc[2 + m] + k_even * fall[m + j]
                            acc[4 + m] = acc[4 + m] + k_odd * next_fall[m + j]
                        p = both[h][0] * odd[j] + both[h][1] * odd[j + 1]
                        parts.append(p + (mine[h][0] * fall[j] + mine[h][2] * fall[j + 1]))
                        parts.append(p - (mine[h][1] * next_fall[j] + mine[h][3] * next_fall[j + 1]))
                    grad[h, pl.ds(pl.multiple_of(at, 8), 8), :] = reduce_eight(parts, masks)
                    new += acc
                return tuple(new)

            return lax.fori_loop(0, blocks, one_block, total)

        total = lax.fori_loop(low_tap[e], high_tap[e] + 1, one_lat, (zero,) * 12)
        for h in range(2):
            for t, value in enumerate(combine(total[6 * h:6 * h + 6])):
                conv[h, pl.ds(r * COLS + t, 8, stride=4), :] = value
        return 0

    lax.fori_loop(0, ROWS, conv_row, 0)
    for h in range(2):
        d_mix[h * HALF:(h + 1) * HALF, :] = lax.dot_general(
            conv[h].astype(bf16), cot_ref[...], (((0,), (0,)), ((), ())), preferred_element_type=f32
        )

    d_out[...] = jnp.zeros_like(d_out)
    d_hid[...] = jnp.zeros_like(d_hid)
    d_small[...] = jnp.zeros_like(d_small)

    def adjoint(g, _):
        raw = []
        pos = [jnp.minimum(GROUP * g + q, own_count - 1) for q in range(GROUP)]
        rows = [slot_row[n] for n in pos]
        for q in range(GROUP):
            i = grid_row(place_ref, rows[q])
            w = lon_of(place_ref, i)
            norm = tab_ref[2, i]
            limit = jnp.where(GROUP * g + q < own_count, 2 * w, -1)
            at = pl.multiple_of(pos[q] * TAPS, 8)
            part = jnp.concatenate([grad[0, pl.ds(at, TAPS), :], grad[1, pl.ds(at, TAPS), :]], axis=1)
            raw.append(jnp.where(tap_index <= limit, part * norm, 0.0))
        raw = jnp.concatenate(raw, axis=0)
        raw_low = raw.astype(bf16)
        h1 = h1_ref[g]
        h2 = h2_ref[g]
        rows_by_rows = (((0,), (0,)), ((), ()))
        d_out[...] += lax.dot_general(h2, raw_low, rows_by_rows, preferred_element_type=f32)
        d_small[5:6, :] += jnp.sum(raw, axis=0, keepdims=True)
        gp = lax.dot_general(
            raw_low, weight_ref[1], (((1,), (1,)), ((), ())), preferred_element_type=f32
        ) * c2_ref[g]
        gp_low = gp.astype(bf16)
        d_hid[...] += lax.dot_general(h1, gp_low, rows_by_rows, preferred_element_type=f32)
        d_small[4:5, :] += jnp.sum(gp, axis=0, keepdims=True)
        gf = lax.dot_general(
            gp_low, weight_ref[0], (((1,), (1,)), ((), ())), preferred_element_type=f32
        )
        for q in range(GROUP):
            e = rows[q]
            i = grid_row(place_ref, e)
            w = lon_of(place_ref, i)
            a = slot_tap[pos[q]]
            t = a + HLAT
            c1 = cos_lon[e - HLAT] * cos_lat[e - HLAT, pl.ds(t, 1), :] - sin_lon[e - HLAT] * sin_lat[e - HLAT, pl.ds(t, 1), :]
            gq = gf[q * TAPS:(q + 1) * TAPS] * c1
            lon = (tap_index - w).astype(f32) * tab_ref[0, i]
            total = jnp.sum(gq, axis=0, keepdims=True)
            d_small[0:1, :] += jnp.sum(gq * lon, axis=0, keepdims=True)
            d_small[1:2, :] += total * (a.astype(f32) * tab_ref[1, i])
            d_small[2:3, :] += total * tab_ref[3, i]
            d_small[3:4, :] += total
        return 0

    lax.fori_loop(0, (own_count + GROUP - 1) // GROUP, adjoint, 0)
    d_small[0:4, :] = d_small[0:4, :] * 30.0
    d_side[...] = jnp.transpose(d_small[...])
    for target, half in ((keep_ref, core), (send_ref, 1 - core)):
        rows = pl.ds(pl.multiple_of(half * HALF, HALF), HALF)
        for q, source in enumerate((d_mix, d_hid, d_out, d_side)):
            part = source[rows, :] * inverse
            target[:, q * C:q * C + part.shape[1]] = part.astype(bf16)


def back_body(half, place_ref, cots_ref, packed, *rest):
    first_ref = rest[0] if half else None
    gfield_ref, slot_row, slot_tap, first_slot, low_tap, high_tap, line, window, change, kern, ksum, back = rest[half:]
    _, slot_count = number_slots(place_ref, slot_row, slot_tap, first_slot, low_tap, high_tap)

    def lay(g, _):
        lay_taps(g, packed[g, :, half * HALF:(half + 1) * HALF], kern, ksum)
        return 0

    lax.fori_loop(0, (slot_count + GROUP - 1) // GROUP, lay, 0)
    def reader(n):
        return lambda part, row, lanes: cots_ref[n, part, row, :, lanes]

    build_windows(place_ref, reader(0), reader(1), reader(2), (half,), 8, line, window, change)
    zero = jnp.zeros((8, HALF), f32)

    def back_row(r, _):
        def one_source(e, total):
            a = r + HLAT - e
            i = safe_row(place_ref, e)
            w = lon_of(place_ref, i)
            live = jnp.logical_and(in_grid(place_ref, e), jnp.abs(a) <= lat_of(place_ref, i))
            blocks = jnp.where(live, (2 * w + 8) // 8, 0)
            slot = first_slot[e] + a

            def one_block(b, total):
                start = HLON + 1 + w - 8 * b
                at = slot * TAPS + 8 * b
                pair = slot * PAIRS + 4 * b
                acc = list(total)
                odd, fall, next_fall = taps_of(window, change, e, 0, start)
                for j in range(4):
                    k_sum = row_of(ksum, 0, pair + 3 - j)
                    k_even = row_of(kern, 0, at + 7 - 2 * j)
                    k_odd = row_of(kern, 0, at + 6 - 2 * j)
                    for m in range(2):
                        acc[m] = acc[m] + k_sum * odd[m + j]
                        acc[2 + m] = acc[2 + m] + k_even * fall[m + j]
                        acc[4 + m] = acc[4 + m] + k_odd * next_fall[m + j]
                return tuple(acc)

            return lax.fori_loop(0, blocks, one_block, total)

        total = lax.fori_loop(r, r + TLAT, one_source, (zero,) * 6)
        for t, value in enumerate(combine(total)):
            back[pl.ds(r * COLS + t, 8, stride=4), :] = value
        return 0

    lax.fori_loop(0, ROWS, back_row, 0)
    if half:
        gfield_ref[:, :HALF] = first_ref[...]
        gfield_ref[:, HALF:] = back[...].astype(bf16)
    else:
        gfield_ref[...] = back[...].astype(bf16)


def unpack_body(place_ref, own_ref, other_ref, mix_ref, hid_ref, out_ref, first_ref, fb_ref, hb_ref, ob_ref, side):
    core = place_ref[1]
    for source, half in ((own_ref, core), (other_ref, 1 - core)):
        rows = pl.ds(pl.multiple_of(half * HALF, HALF), HALF)
        for q, target in enumerate((mix_ref, hid_ref, out_ref)):
            target[rows, :] = source[:, q * C:(q + 1) * C].astype(f32)
        side[rows, :] = source[:, 3 * C:].astype(f32)
    small = jnp.transpose(side[...])
    first_ref[...] = small[0:3]
    fb_ref[...] = small[3:4]
    hb_ref[...] = small[4:5]
    ob_ref[...] = small[5:6]


def unpack(place, own, other):
    vmem = pl.BlockSpec(memory_space=pltpu.VMEM)
    square = jax.ShapeDtypeStruct((C, C), f32)
    line = jax.ShapeDtypeStruct((1, C), f32)
    return pl.pallas_call(
        unpack_body,
        out_shape=(square, square, square, jax.ShapeDtypeStruct((3, C), f32), line, line, line),
        in_specs=[pl.BlockSpec(memory_space=pltpu.SMEM)] + [vmem] * 2,
        out_specs=(vmem,) * 7,
        scratch_shapes=[pltpu.VMEM((C, HALF), f32)],
        compiler_params=pltpu.CompilerParams(vmem_limit_bytes=8 * 1024 * 1024),
        name="unpack",
    )(place, own, other)


def slot_scratch():
    return [
        pltpu.SMEM((SLOTS + 8,), jnp.int32),
        pltpu.SMEM((SLOTS + 8,), jnp.int32),
        pltpu.SMEM((16,), jnp.int32),
        pltpu.SMEM((16,), jnp.int32),
        pltpu.SMEM((16,), jnp.int32),
    ]


def gradient_pass(place, table, here, inner, outer, cotangent, weights, saved):
    smem = pl.BlockSpec(memory_space=pltpu.SMEM)
    vmem = pl.BlockSpec(memory_space=pltpu.VMEM)
    return pl.pallas_call(
        gradient_body,
        out_shape=(
            jax.ShapeDtypeStruct((C // 2, PACK), bf16),
            jax.ShapeDtypeStruct((C // 2, PACK), bf16),
            jax.ShapeDtypeStruct((3, 3, ROWS, COLS, C), bf16),
        ),
        in_specs=[smem] * 2 + [vmem] * 14,
        out_specs=(vmem,) * 3,
        scratch_shapes=slot_scratch() + [
            pltpu.VMEM((2, LINE, HALF), f32),
            pltpu.VMEM((EXT, 2, WIN, 8, HALF), f32),
            pltpu.VMEM((EXT, 2, WIN, 8, HALF), f32),
            pltpu.VMEM((2, ROWS * COLS, HALF), f32),
            pltpu.VMEM((2, OWN * TAPS, HALF), f32),
            pltpu.VMEM((2, ROWS * COLS, HALF), f32),
            pltpu.VMEM((C, C), f32),
            pltpu.VMEM((C, C), f32),
            pltpu.VMEM((C, C), f32),
            pltpu.VMEM((HALF, C), f32),
            pltpu.VMEM((C, HALF), f32),
        ],
        compiler_params=pltpu.CompilerParams(vmem_limit_bytes=26 * 1024 * 1024),
        cost_estimate=pl.CostEstimate(flops=9_000_000_000, bytes_accessed=20_000_000, transcendentals=0),
        name="gradient_pass",
    )(place, table, here, inner, outer, cotangent, weights, *saved)


def back_pass(half, place, cots, packed, *first):
    smem = pl.BlockSpec(memory_space=pltpu.SMEM)
    vmem = pl.BlockSpec(memory_space=pltpu.VMEM)
    return pl.pallas_call(
        functools.partial(back_body, half),
        out_shape=jax.ShapeDtypeStruct((ROWS * COLS, C if half else HALF), bf16),
        in_specs=[smem] + [vmem] * (2 + half),
        out_specs=vmem,
        scratch_shapes=slot_scratch() + [
            pltpu.VMEM((1, LINE, HALF), f32),
            pltpu.VMEM((EXT, 1, WIN, 8, HALF), f32),
            pltpu.VMEM((EXT, 1, WIN, 8, HALF), f32),
            pltpu.VMEM((1, SLOTS * TAPS, HALF), f32),
            pltpu.VMEM((1, SLOTS * PAIRS, HALF), f32),
            pltpu.VMEM((ROWS * COLS, HALF), f32),
        ],
        compiler_params=pltpu.CompilerParams(vmem_limit_bytes=16 * 1024 * 1024),
        cost_estimate=pl.CostEstimate(flops=2_500_000_000, bytes_accessed=4_000_000, transcendentals=0),
        name=f"back_pass_{half}",
    )(place, cots, packed, *first)


def core_add_body(keep_ref, other_ref, total_ref):
    total_ref[...] = (keep_ref[...].astype(f32) + other_ref[...].astype(f32)).astype(bf16)


def core_add(keep, other):
    vmem = pl.BlockSpec(memory_space=pltpu.VMEM)
    return pl.pallas_call(
        core_add_body,
        out_shape=jax.ShapeDtypeStruct(keep.shape, bf16),
        in_specs=[vmem] * 2,
        out_specs=vmem,
        compiler_params=pltpu.CompilerParams(vmem_limit_bytes=4 * 1024 * 1024),
        name="core_add",
    )(keep, other)


def swap(block, axis, pairs):
    return lax.ppermute(block, axis, pairs)


LAT_INNER = [(i, i ^ 1) for i in range(8)]
LAT_OUTER = [(i, i + 1 if i % 2 else i - 1) for i in range(1, 7)]
LON_INNER = [(i, i ^ 1) for i in range(32)]
LON_OUTER = [(i, (i + 1 if i % 2 else i - 1) % 32) for i in range(32)]
PLANE = ("y", "x_low", "x_high")


def spread(block, axis):
    return lax.all_to_all(block, axis, 0, 0, tiled=True)


LAT = ("y", "x_low")
LON = ("z", "x_high", "core")
CORE = [(0, 1), (1, 0)]


def beside(block):
    return jnp.stack((block, swap(block, LAT, LAT_INNER), swap(block, LAT, LAT_OUTER)), axis=0)


def around(here):
    return here, swap(here, LON, LON_INNER), swap(here, LON, LON_OUTER)


def z_add(total, bits):
    return total + swap(total, "z", [(i, i ^ bits) for i in range(8)])


def shards(
    field, cotangent, mix_weight, first_weight, first_bias, hidden_weight, hidden_bias,
    output_weight, output_bias, lon_half, lat_half,
):
    flat_cot = cotangent.reshape(-1, C)
    mixed = lax.dot_general(
        flat_cot, mix_weight, (((1,), (1,)), ((), ())), preferred_element_type=f32
    ).astype(bf16)
    parts = around(beside(jnp.stack((field, mixed.reshape(ROWS, COLS, C)), axis=0)))
    lat = lax.axis_index("y") * 2 + lax.axis_index("x_low")
    place = jnp.stack((lat * ROWS, lax.axis_index("core"), lat % 2)).astype(jnp.int32)
    place = jnp.concatenate((place, lon_half, lat_half))
    table = tables(lon_half, lat_half)
    vectors = jnp.concatenate((first_weight, jnp.stack((first_bias, hidden_bias, output_bias))), axis=0)
    weights = jnp.stack((hidden_weight, output_weight))
    kern, ksum, packed, *saved = network_pass(place, table, vectors, weights)
    keep, send, cots = gradient_pass(place, table, *parts, flat_cot, weights, (kern, ksum, *saved))
    total = core_add(keep, swap(send, "core", CORE))
    total, cots = lax.optimization_barrier((total, cots))
    total = spread(total.reshape(16, 8, PACK), PLANE)
    back = back_pass(0, place, cots, packed)
    total, back = lax.optimization_barrier((total, back))
    total = jnp.sum(total.astype(f32), axis=0)
    for bits in (1, 2, 6):
        total = z_add(total, bits)
    total, cots = lax.optimization_barrier((total.astype(bf16), cots))
    own = spread(jnp.broadcast_to(total[None], (16, 8, PACK)), PLANE).reshape(HALF, PACK)
    back = back_pass(1, place, cots, packed, back)
    own, back = lax.optimization_barrier((own, back))
    mix, hid, out, first, fb, hb, ob = unpack(place, own, swap(own, "core", CORE))
    return (
        back.reshape(ROWS, COLS, C), mix, first, fb.reshape(C), hid, hb.reshape(C), out, ob.reshape(C),
    )


def solution(mesh):
    split = Mesh(mesh.devices.reshape(8, 2, 2, 4, 2), ("z", "x_high", "core", "y", "x_low"))
    grid = P(LAT, LON, None)
    in_specs = (grid, grid) + (P(),) * 9
    out_specs = (grid,) + (P(),) * 7
    return jax.shard_map(shards, mesh=split, in_specs=in_specs, out_specs=out_specs, check_vma=False)
```
